32 devices in a mesh: role: 2 (over y), proto: 8 (over z, x), crop: 2 (over core).
Axes of the slice: x: 2, y: 2, z: 4, core: 2. Of those that a mesh axis runs over, the one named last changes fastest.
Arguments:
- embeddings: bfloat16 [2, 1024, 512], P('role', 'crop'), may hold values from -1 to 1, as said below
- weights: bfloat16 [2, 512, 262144], P('role', None, 'proto'), may hold values from -1 to 1, as said below
Outputs:
- weight_grad: bfloat16 [2, 2, 128, 262144], P('crop', 'role', None, 'proto')
- embed_grad: bfloat16 [2, 512, 512], P('crop', 'proto', 'role')
The draws below stay inside these ranges and needn't reach their ends.
Inputs may be any that keep to these rules, and one draw needn't show every extreme that they name: `embeddings`: each crop's row has unit Euclidean length before rounding to bfloat16. `weights`: each prototype column has unit Euclidean length before rounding to bfloat16.
All inputs are finite; a program needn't handle non-finite values.
Results may differ from the reference program's by a relative error of at most 0.001.
The reference program's roundings to bfloat16 on the way (of `targets` and `logit_grads`) count: a program that leaves them out, or rounds other values in their place, can miss the bound.
Values may be sent and summed in bfloat16 or wider, within the bound.
No kernel may reach another device: no remote copies, remote signals or barrier semaphores. Data moves between devices by JAX's collectives and lax.ppermute only.
A program may use at most 256 MiB of HBM per device.

```python
import jax
import jax.numpy as jnp
from jax import lax

D = 512
PROTOS = 262144
CROPS = 1024
ITERS = 3


cluster_count = 4


def unit_rows(values):
    return values / jnp.sqrt(jnp.sum(values * values, axis=1, keepdims=True))


def rough_rows(row_key, row_total):
    values = jax.random.normal(row_key, (row_total, D), jnp.float32)
    return unit_rows(values)


def group_centers(key, which_group):
    centers = jax.random.normal(jax.random.fold_in(key, 71 + which_group), (cluster_count, D), jnp.float32)
    return unit_rows(centers)


def draw_weights(key, part):
    matrices = []
    for which_group in range(2):
        centers = group_centers(key, which_group)
        member = jax.random.randint(jax.random.fold_in(key, 31 + which_group), (PROTOS,), 0, cluster_count, jnp.int32)
        columns = rough_rows(jax.random.fold_in(key, 61 + which_group), PROTOS)
        toward = jnp.take(centers, member, axis=0)
        columns = columns + 0.8 * toward
        matrices.append(unit_rows(columns).T.astype(jnp.bfloat16))
    return jnp.stack(matrices)


def draw_embeddings(key, part):
    groups = []
    for which_group in range(2):
        centers = group_centers(key, which_group)
        member = jnp.maximum(jax.random.randint(jax.random.fold_in(key, 41 + which_group), (CROPS,), -cluster_count, cluster_count, jnp.int32), 0)
        toward = jnp.take(centers, member, axis=0)
        noise = rough_rows(jax.random.fold_in(key, 51 + which_group), CROPS)
        mixed = 0.5 * toward + 0.866 * noise
        groups.append(unit_rows(mixed))
    return jnp.stack(groups).astype(jnp.bfloat16)


def setup_inputs(seed: int = 0) -> dict:
    key_of = jax.random.split(jax.random.key(seed), 3)
    embeddings = draw_embeddings(jax.random.fold_in(key_of[2], 71), 0)
    weights = draw_weights(jax.random.fold_in(key_of[2], 71), 0)
    return dict(embeddings=embeddings, weights=weights)


def log_sum(numeric_items, along):
    return jnp.log(jnp.sum(jnp.exp(numeric_items), axis=along, keepdims=True))


def reference(embeddings, weights):
    teacher_scores = jnp.dot(embeddings[0], weights[0], preferred_element_type=jnp.float32)
    student_scores = jnp.dot(embeddings[1], weights[1], preferred_element_type=jnp.float32)
    teacher_logits = teacher_scores / 0.07
    student_logits = student_scores / 0.1
    row_shift = jnp.zeros((CROPS, 1), jnp.float32)
    column_shift = jnp.zeros((1, PROTOS), jnp.float32)
    for iteration in range(ITERS):
        column_shift = -log_sum(teacher_logits + row_shift, 0)
        row_shift = -log_sum(teacher_logits + column_shift, 1)
    targets = jnp.exp(teacher_logits + column_shift + row_shift).astype(jnp.bfloat16)
    student_exp = jnp.exp(student_logits)
    student_probs = student_exp / jnp.sum(student_exp, axis=1, keepdims=True)
    logit_grads = ((student_probs - targets.astype(jnp.float32)) / 0.1).astype(jnp.bfloat16)
    weight_full = lax.dot_general(embeddings[1], logit_grads, (((0,), (0,)), ((), ())), preferred_element_type=jnp.float32)
    embed_full = lax.dot_general(logit_grads, weights[1], (((1,), (1,)), ((), ())), preferred_element_type=jnp.float32)
    weight_grad = weight_full.astype(jnp.bfloat16).reshape(2, 2, D // 4, PROTOS)
    embed_grad = embed_full.astype(jnp.bfloat16).reshape(2, CROPS // 2, D)
    return weight_grad, embed_grad
```

```python
import functools

import jax
import jax.numpy as jnp
from jax import lax
from jax.experimental import pallas as pl
from jax.experimental.pallas import tpu as pltpu
from jax.sharding import PartitionSpec as P

ITERS = 3
LOG2E = 1.4426950408889634
CHUNKS = 4
ROWS = 256
NT = (((1,), (1,)), ((), ()))


def whole(shape):
    return pl.BlockSpec(shape, lambda *_: (0,) * len(shape), pipeline_mode=pl.Buffered(1))


def cost(flops, bytes_accessed, transcendentals):
    return pl.CostEstimate(
        flops=flops, bytes_accessed=bytes_accessed, transcendentals=transcendentals
    )


def lane_tiles(value, width):
    return jnp.concatenate([value] * (width // value.shape[1]), axis=1)


def copy_body(places, source, target):
    target[...] = source[...]


def columns_of(places, matrix, chunk, width):
    depth = matrix.shape[0]
    tile = min(width, 1024)
    tiles = width // tile
    return pl.pallas_call(
        copy_body,
        out_shape=jax.ShapeDtypeStruct((depth, width), matrix.dtype),
        grid_spec=pltpu.PrefetchScalarGridSpec(
            num_scalar_prefetch=1,
            grid=(tiles,),
            in_specs=[
                pl.BlockSpec(
                    (depth, tile),
                    lambda t, places: (0, (places[2] * CHUNKS + chunk) * tiles + t),
                )
            ],
            out_specs=pl.BlockSpec((depth, tile), lambda t, places: (0, t)),
        ),
        cost_estimate=cost(0, 4 * depth * width, 0),
        name="columns_of",
    )(places, matrix)


def pass_body(places, scale, embed, weight, row_scale, row_sums, column_scale, kept, sums):
    step = pl.program_id(0)
    crops = embed.shape[0]
    width = weight.shape[1]

    @pl.when(step == 0)
    def _():
        sums[...] = jnp.zeros_like(sums)

    block = weight[...]
    total = jnp.zeros((8, width), jnp.float32)
    for start in range(0, crops, ROWS):
        rows = pl.ds(start, ROWS)
        scores = jnp.dot(embed[rows, :], block, preferred_element_type=jnp.float32)
        powers = jnp.exp2(scores * scale[0])
        kept[rows, :] = powers
        scaled = powers * lane_tiles(row_scale[rows, :], width)
        total += jnp.sum(scaled.reshape(ROWS // 8, 8, width), axis=0)
    column_sum = jnp.sum(total, axis=0, keepdims=True)
    factor = jnp.where(places[0] == 1, 1.0, 1.0 / column_sum)
    column_scale[...] = factor
    for start in range(0, crops, ROWS):
        rows = pl.ds(start, ROWS)
        part = kept[rows, :] * factor
        folded = part[:, :128]
        for lane in range(128, width, 128):
            folded += part[:, lane : lane + 128]
        sums[rows, :] += folded

    @pl.when(step == pl.num_programs(0) - 1)
    def _():
        row_sums[...] = lax.dot_general(
            jnp.ones((8, 128), jnp.float32),
            sums[...],
            NT,
            precision=lax.Precision.HIGHEST,
            preferred_element_type=jnp.float32,
        )


def sinkhorn_pass(places, scale, embed, weight, row_scale):
    crops, depth = embed.shape
    half = weight.shape[1] // 2
    tile = min(512, half)
    tiles = half // tile
    return pl.pallas_call(
        pass_body,
        out_shape=(
            jax.ShapeDtypeStruct((8, crops), jnp.float32),
            jax.ShapeDtypeStruct((1, half), jnp.float32),
        ),
        grid_spec=pltpu.PrefetchScalarGridSpec(
            num_scalar_prefetch=1,
            grid=(tiles,),
            in_specs=[
                pl.BlockSpec(memory_space=pltpu.SMEM),
                whole((crops, depth)),
                pl.BlockSpec((depth, tile), lambda t, places: (0, places[3] * tiles + t)),
                whole((crops, 128)),
            ],
            out_specs=[
                whole((8, crops)),
                pl.BlockSpec((1, tile), lambda t, places: (0, t)),
            ],
            scratch_shapes=[
                pltpu.VMEM((crops, tile), jnp.float32),
                pltpu.VMEM((crops, 128), jnp.float32),
            ],
        ),
        cost_estimate=cost(2 * crops * depth * half, 2 * depth * half, crops * half),
        name="sinkhorn_pass",
    )(places, scale, embed, weight, row_scale)


def grads_body(
    places,
    teacher_embed,
    student_embed,
    turned,
    own,
    arrived,
    row_scale,
    inverse_sum,
    column_scale,
    embed_start,
    kept_piece,
    crop_piece,
    role_piece,
    diagonal_piece,
    embed_total,
    logit_grads,
):
    step = pl.program_id(0)
    crops = teacher_embed.shape[0]
    width = own.shape[1]
    quarter = turned.shape[0] // 4

    @pl.when(step == 0)
    def _():
        embed_total[...] = embed_start[...]

    def tile(teacher, student):
        teacher_block = teacher[...]
        student_block = student[...]
        factor = column_scale[...]
        for start in range(0, crops, ROWS):
            rows = pl.ds(start, ROWS)
            teacher_scores = jnp.dot(
                teacher_embed[rows, :], teacher_block, preferred_element_type=jnp.float32
            )
            student_scores = jnp.dot(
                student_embed[rows, :], student_block, preferred_element_type=jnp.float32
            )
            targets = (
                jnp.exp2(teacher_scores * (LOG2E / 0.07))
                * factor
                * lane_tiles(row_scale[rows, :], width)
            ).astype(jnp.bfloat16)
            probs = jnp.exp2(student_scores * (LOG2E / 0.1)) * lane_tiles(
                inverse_sum[rows, :], width
            )
            grads = ((probs - targets.astype(jnp.float32)) * 10.0).astype(jnp.bfloat16)
            logit_grads[rows, :] = grads
            embed_total[rows, :] += lax.dot_general(
                grads, student_block, NT, preferred_element_type=jnp.float32
            )
        pieces = (kept_piece, crop_piece, role_piece, diagonal_piece)
        for place, piece in enumerate(pieces):
            piece[...] = jnp.dot(
                turned[pl.ds(place * quarter, quarter), :],
                logit_grads[...],
                preferred_element_type=jnp.float32,
            ).astype(piece.dtype)

    @pl.when(places[0] == 0)
    def _():
        tile(own, arrived)

    @pl.when(places[0] == 1)
    def _():
        tile(arrived, own)


def gradients(places, chunk, embeds, turned, own, arrived, scales, column_scale, embed_start):
    crops, depth = embeds[0].shape
    width = arrived.shape[1]
    tile = min(512, width)
    tiles = width // tile
    quarter = depth // 4
    piece = jax.ShapeDtypeStruct((quarter, width), jnp.bfloat16)
    piece_spec = pl.BlockSpec((quarter, tile), lambda t, places: (0, t))
    return pl.pallas_call(
        grads_body,
        out_shape=(piece,) * 4 + (jax.ShapeDtypeStruct((crops, depth), jnp.float32),),
        grid_spec=pltpu.PrefetchScalarGridSpec(
            num_scalar_prefetch=1,
            grid=(tiles,),
            in_specs=[
                whole((crops, depth)),
                whole((crops, depth)),
                whole((depth, crops)),
                pl.BlockSpec(
                    (depth, tile),
                    lambda t, places: (0, (places[1] * CHUNKS + chunk) * tiles + t),
                ),
                pl.BlockSpec((depth, tile), lambda t, places: (0, t)),
                whole((crops, 128)),
                whole((crops, 128)),
                pl.BlockSpec((1, tile), lambda t, places: (0, chunk * tiles + t)),
                whole((crops, depth)),
            ],
            out_specs=[piece_spec] * 4 + [whole((crops, depth))],
            scratch_shapes=[pltpu.VMEM((crops, tile), jnp.bfloat16)],
        ),
        cost_estimate=cost(
            8 * crops * depth * width, 6 * depth * width + 8 * crops * depth, 2 * crops * width
        ),
        name="gradients",
    )(
        places,
        *embeds,
        turned,
        own,
        arrived,
        *scales,
        column_scale,
        embed_start,
    )


def place_body(places, kept_piece, crop_piece, role_piece, diagonal_piece, before, after):
    step = pl.program_id(0)
    for place, piece in enumerate((kept_piece, crop_piece, role_piece, diagonal_piece)):

        @pl.when(step == place)
        def _(piece=piece):
            after[...] = piece[...]


def placed_pieces(places, chunk, pieces, before, block_width):
    rows, width = pieces[0].shape
    out_shape = jax.ShapeDtypeStruct((rows, block_width), pieces[0].dtype)
    aliases = {} if before is None else {5: 0}
    body = place_body
    if before is None:
        body = lambda places, *refs: place_body(places, *refs[:4], None, refs[4])
    operands = [places, *pieces] + ([] if before is None else [before])
    specs = [whole((rows, width))] * 4
    if before is not None:
        specs = specs + [pl.BlockSpec(memory_space=pl.ANY)]
    return pl.pallas_call(
        body,
        out_shape=out_shape,
        grid_spec=pltpu.PrefetchScalarGridSpec(
            num_scalar_prefetch=1,
            grid=(4,),
            in_specs=specs,
            out_specs=pl.BlockSpec(
                (rows, width), lambda t, places: (0, places[4 + t] * CHUNKS + chunk)
            ),
        ),
        input_output_aliases=aliases,
        cost_estimate=cost(0, 16 * rows * width, 0),
        name="placed_pieces",
    )(*operands)


def swapped(value, *axes):
    if axes == ("role", "crop"):
        return lax.ppermute(value, axes, [(0, 3), (1, 2), (2, 1), (3, 0)])
    return lax.ppermute(value, axes[0], [(0, 1), (1, 0)])


def both_crops(mine, other, crop_place):
    first = jnp.where(crop_place == 0, mine, other)
    second = jnp.where(crop_place == 0, other, mine)
    return jnp.concatenate([first, second], axis=0)


def per_device(embeddings, weights):
    role_place = lax.axis_index("role")
    crop_place = lax.axis_index("crop")
    own_embed = embeddings[0]
    own_weight = weights[0]
    crops = 2 * own_embed.shape[0]
    depth = own_embed.shape[1]
    block_width = own_weight.shape[1]
    quarter_width = block_width // 4
    chunk_width = quarter_width // CHUNKS
    teaches = role_place == 0

    own_quarter = 2 * crop_place + role_place
    partner_quarter = 2 * crop_place + 1 - role_place
    order = [own_quarter, own_quarter ^ 2, own_quarter ^ 1, own_quarter ^ 3]
    places = jnp.stack([role_place, own_quarter, partner_quarter, crop_place] + order).astype(
        jnp.int32
    )

    crop_embed = swapped(own_embed, "crop")
    arrived = [
        swapped(columns_of(places, own_weight, chunk, chunk_width), "role")
        for chunk in range(CHUNKS)
    ]
    own_all = both_crops(own_embed, crop_embed, crop_place)
    role_embed = swapped(own_embed, "role")
    diagonal_embed = swapped(role_embed, "crop")
    other_all = both_crops(role_embed, diagonal_embed, crop_place)

    scale = jnp.where(teaches, LOG2E / 0.07, LOG2E / 0.1).astype(jnp.float32).reshape(1)
    row_scale = jnp.ones((crops, 128), jnp.float32)
    for iteration in range(ITERS):
        row_sums, column_scale = sinkhorn_pass(places, scale, own_all, own_weight, row_scale)
        inverse = 1.0 / lax.psum(row_sums[0], ("proto", "crop"))
        row_scale = jnp.broadcast_to(inverse[:, None], (crops, 128))

    halves = column_scale.reshape(2, quarter_width)
    partner_columns = lax.dynamic_index_in_dim(halves, 1 - role_place, 0)
    own_columns = lax.dynamic_index_in_dim(halves, role_place, 0)
    got_columns = swapped(partner_columns, "role")
    got_inverse = swapped(inverse, "role")
    columns = jnp.where(teaches, own_columns, got_columns)
    got_scale = jnp.broadcast_to(got_inverse[:, None], (crops, 128))
    scales = (
        jnp.where(teaches, row_scale, got_scale),
        jnp.where(teaches, got_scale, row_scale),
    )
    embeds = (jnp.where(teaches, own_all, other_all), jnp.where(teaches, other_all, own_all))
    blocks = embeds[1].T.reshape(4, depth // 4, crops)
    turned = jnp.concatenate(
        [lax.dynamic_index_in_dim(blocks, place, 0, keepdims=False) for place in order], axis=0
    )

    embed_part = jnp.zeros((crops, depth), jnp.float32)
    result = None
    for chunk in range(CHUNKS):
        kept_piece, crop_piece, role_piece, diagonal_piece, embed_part = gradients(
            places, chunk, embeds, turned, own_weight, arrived[chunk], scales, columns, embed_part
        )
        pieces = (
            kept_piece,
            swapped(crop_piece, "crop"),
            swapped(role_piece, "role"),
            swapped(diagonal_piece, "role", "crop"),
        )
        result = placed_pieces(places, chunk, pieces, result, block_width)
    weight_block = result.reshape(1, 1, depth // 4, block_width)

    summed = lax.psum_scatter(embed_part, ("crop", "proto"), scatter_dimension=0, tiled=True)
    sides = summed.reshape(summed.shape[0], 2, depth // 2)
    theirs = lax.dynamic_index_in_dim(sides, 1 - role_place, 1, keepdims=False)
    mine = lax.dynamic_index_in_dim(sides, role_place, 1, keepdims=False)
    embed_block = (mine + swapped(theirs, "role")).astype(jnp.bfloat16)[None]
    return (weight_block, embed_block)


def solution(mesh):
    placed = (P("role", "crop", None), P("role", None, "proto"))
    return jax.shard_map(
        per_device,
        mesh=mesh,
        in_specs=placed,
        out_specs=(P("crop", "role", None, "proto"), P("crop", "proto", "role")),
        check_vma=False,
    )
```

```python
import functools
import math

import jax
import jax.numpy as jnp
from jax import lax
from jax.experimental import pallas as pl
from jax.experimental.pallas import tpu as pltpu
from jax.sharding import PartitionSpec as P


ITERS = 3
LOG2E = 1.4426950408889634
SHARES = (4, 4, 5, 3)
CHUNKS = len(SHARES)
GRAD_ORDER = (1, 2, 0, 3)
ROWS = 256
NT = (((1,), (1,)), ((), ()))


def whole(shape):
    return pl.BlockSpec(shape, lambda *_: (0,) * len(shape), pipeline_mode=pl.Buffered(1))


def cost(flops, bytes_accessed, transcendentals):
    return pl.CostEstimate(
        flops=flops, bytes_accessed=bytes_accessed, transcendentals=transcendentals
    )


def tile_width(quarter_width):
    return 512 if quarter_width % 8192 == 0 else 128


def chunk_tiles(quarter_width):
    tiles = quarter_width // tile_width(quarter_width)
    edges = [-(-tiles * sum(SHARES[:n]) // sum(SHARES)) for n in range(CHUNKS + 1)]
    return [(begin, end - begin) for begin, end in zip(edges, edges[1:])]


def lane_tiles(value, width):
    return jnp.concatenate([value] * (width // value.shape[1]), axis=1)


def copy_body(places, source, target):
    target[...] = source[...]


def columns_of(places, matrix, chunk):
    depth = matrix.shape[0]
    quarter_width = matrix.shape[1] // 4
    tile = tile_width(quarter_width)
    tiles = quarter_width // tile
    begin, count = chunk_tiles(quarter_width)[chunk]
    width = count * tile
    return pl.pallas_call(
        copy_body,
        out_shape=jax.ShapeDtypeStruct((depth, width), matrix.dtype),
        grid_spec=pltpu.PrefetchScalarGridSpec(
            num_scalar_prefetch=1,
            grid=(count,),
            in_specs=[
                pl.BlockSpec(
                    (depth, tile), lambda t, places: (0, places[2] * tiles + begin + t)
                )
            ],
            out_specs=pl.BlockSpec((depth, tile), lambda t, places: (0, t)),
        ),
        cost_estimate=cost(0, 4 * depth * width, 0),
        name="columns_of",
    )(places, matrix)


def reciprocal_rows(parts, crops):
    total = parts[0][...]
    for part in parts[1:]:
        total = total + part[...]
    return jnp.transpose(jnp.broadcast_to(1.0 / total, (128, crops)))


def pass_body(first, nparts, tiles, places, scale, embed, weight, *refs):
    parts, refs = refs[:nparts], refs[nparts:]
    row_sums, own_factor, partner_factor = refs[:3]
    sent = refs[3:-3] if first else ()
    kept, sums, row_scale = refs[-3:]
    step = pl.program_id(0)
    crops = embed.shape[0]
    width = weight.shape[1]

    @pl.when(step == 0)
    def _():
        sums[...] = jnp.zeros_like(sums)
        if not first:
            row_scale[...] = reciprocal_rows(parts, crops)

    block = weight[...]
    total = jnp.zeros((8, width), jnp.float32)
    for start in range(0, crops, ROWS):
        rows = pl.ds(start, ROWS)
        scores = jnp.dot(embed[rows, :], block, preferred_element_type=jnp.float32)
        powers = jnp.exp2(scores * scale[0])
        kept[rows, :] = powers
        if not first:
            powers = powers * lane_tiles(row_scale[rows, :], width)
        total += jnp.sum(powers.reshape(ROWS // 8, 8, width), axis=0)
    column_sum = jnp.sum(total, axis=0, keepdims=True)
    factor = jnp.where(places[0] == 1, 1.0, 1.0 / column_sum)
    owned = step // tiles == places[0]

    @pl.when(owned)
    def _():
        own_factor[...] = factor

    @pl.when(jnp.logical_not(owned))
    def _():
        partner_factor[...] = factor

    here = lax.rem(step, tiles)
    for (begin, count), piece in zip(chunk_tiles(tiles * width)[1:], sent):

        @pl.when(jnp.logical_not(owned) & (here >= begin) & (here < begin + count))
        def _(piece=piece):
            piece[...] = block

    for start in range(0, crops, ROWS):
        rows = pl.ds(start, ROWS)
        part = kept[rows, :] * factor
        folded = part[:, :128]
        for lane in range(128, width, 128):
            folded += part[:, lane : lane + 128]
        sums[rows, :] += folded

    @pl.when(step == pl.num_programs(0) - 1)
    def _():
        ones = jnp.ones((8, 128), jnp.float32)
        row_sums[...] = lax.dot_general(
            ones,
            sums[...],
            NT,
            precision=lax.Precision.HIGHEST,
            preferred_element_type=jnp.float32,
        )[:1]


def sinkhorn_pass(places, scale, embed, weight, parts):
    crops, depth = embed.shape
    quarter_width = weight.shape[1] // 4
    tile = tile_width(quarter_width)
    tiles = quarter_width // tile
    first = not parts

    def owner_spec(partner):
        def index(t, places):
            begin = tiles * (1 - places[0] if partner else places[0])
            return (0, jnp.clip(t - begin, 0, tiles - 1))

        return pl.BlockSpec((1, tile), index)

    def sent_spec(begin, count):
        def index(t, places):
            return (0, jnp.clip(t - tiles * (1 - places[0]) - begin, 0, count - 1))

        return pl.BlockSpec((depth, tile), index)

    sent = chunk_tiles(quarter_width)[1:] if first else ()
    factor_shape = jax.ShapeDtypeStruct((1, quarter_width), jnp.float32)
    return pl.pallas_call(
        functools.partial(pass_body, first, len(parts), tiles),
        out_shape=[
            jax.ShapeDtypeStruct((1, crops), jnp.float32),
            factor_shape,
            factor_shape,
            *[jax.ShapeDtypeStruct((depth, count * tile), weight.dtype) for _, count in sent],
        ],
        grid_spec=pltpu.PrefetchScalarGridSpec(
            num_scalar_prefetch=1,
            grid=(2 * tiles,),
            in_specs=[
                pl.BlockSpec(memory_space=pltpu.SMEM),
                whole((crops, depth)),
                pl.BlockSpec((depth, tile), lambda t, places: (0, places[3] * 2 * tiles + t)),
                *[pl.BlockSpec(memory_space=pltpu.VMEM) for _ in parts],
            ],
            out_specs=[
                whole((1, crops)),
                owner_spec(False),
                owner_spec(True),
                *[sent_spec(begin, count) for begin, count in sent],
            ],
            scratch_shapes=[
                pltpu.VMEM((crops, tile), jnp.float32),
                pltpu.VMEM((crops, 128), jnp.float32),
                pltpu.VMEM((crops, 128), jnp.float32),
            ],
        ),
        cost_estimate=cost(
            4 * crops * depth * quarter_width, 4 * depth * quarter_width, 2 * crops * quarter_width
        ),
        name="sinkhorn_pass",
    )(places, scale, embed, weight, *parts)


def scales_body(nparts, places, *refs):
    parts, (got_inverse, own_factor, got_factor) = refs[:nparts], refs[nparts : nparts + 3]
    row_scale, inverse_sum, column_scale = refs[nparts + 3 :]
    crops = got_inverse.shape[1]
    mine = reciprocal_rows(parts, crops)
    theirs = jnp.transpose(jnp.broadcast_to(got_inverse[...], (128, crops)))
    teaches = places[0] == 0
    row_scale[...] = jnp.where(teaches, mine, theirs)
    inverse_sum[...] = jnp.where(teaches, theirs, mine)
    column_scale[...] = jnp.where(teaches, own_factor[...], got_factor[...])


def final_scales(places, parts, got_inverse, own_factor, got_factor):
    crops = got_inverse.shape[1]
    rows = jax.ShapeDtypeStruct((crops, 128), jnp.float32)
    return pl.pallas_call(
        functools.partial(scales_body, len(parts)),
        out_shape=[rows, rows, jax.ShapeDtypeStruct(own_factor.shape, jnp.float32)],
        grid_spec=pltpu.PrefetchScalarGridSpec(
            num_scalar_prefetch=1,
            grid=(1,),
            in_specs=[pl.BlockSpec(memory_space=pltpu.VMEM)] * (len(parts) + 3),
            out_specs=[whole((crops, 128))] * 2 + [whole(own_factor.shape)],
        ),
        cost_estimate=cost(0, 8 * crops * 128, 0),
        name="final_scales",
    )(places, *parts, got_inverse, own_factor, got_factor)


def grads_body(
    places,
    teacher_embed,
    student_embed,
    turned,
    own,
    arrived,
    row_scale,
    inverse_sum,
    column_scale,
    embed_start,
    kept_piece,
    crop_piece,
    role_piece,
    diagonal_piece,
    embed_total,
    logit_grads,
):
    step = pl.program_id(0)
    crops = teacher_embed.shape[0]
    width = own.shape[1]
    quarter = turned.shape[0] // 4

    @pl.when(step == 0)
    def _():
        embed_total[...] = embed_start[...]

    def tile(teacher, student):
        teacher_block = teacher[...]
        student_block = student[...]
        factor = column_scale[...]
        for start in range(0, crops, ROWS):
            rows = pl.ds(start, ROWS)
            teacher_scores = jnp.dot(
                teacher_embed[rows, :], teacher_block, preferred_element_type=jnp.float32
            )
            student_scores = jnp.dot(
                student_embed[rows, :], student_block, preferred_element_type=jnp.float32
            )
            targets = (
                jnp.exp2(teacher_scores * (LOG2E / 0.07))
                * factor
                * lane_tiles(row_scale[rows, :], width)
            ).astype(jnp.bfloat16)
            probs = jnp.exp2(student_scores * (LOG2E / 0.1)) * lane_tiles(
                inverse_sum[rows, :], width
            )
            grads = ((probs - targets.astype(jnp.float32)) * 10.0).astype(jnp.bfloat16)
            logit_grads[rows, :] = grads
            embed_total[rows, :] += lax.dot_general(
                grads, student_block, NT, preferred_element_type=jnp.float32
            )
        pieces = (kept_piece, crop_piece, role_piece, diagonal_piece)
        for place, piece in enumerate(pieces):
            piece[...] = jnp.dot(
                turned[pl.ds(place * quarter, quarter), :],
                logit_grads[...],
                preferred_element_type=jnp.float32,
            ).astype(piece.dtype)

    @pl.when(places[0] == 0)
    def _():
        tile(own, arrived)

    @pl.when(places[0] == 1)
    def _():
        tile(arrived, own)


def gradients(places, chunk, embeds, turned, own, arrived, scales, column_scale, embed_start):
    crops, depth = embeds[0].shape
    width = arrived.shape[1]
    quarter_width = own.shape[1] // 4
    tile = tile_width(quarter_width)
    tiles = quarter_width // tile
    begin, count = chunk_tiles(quarter_width)[chunk]
    quarter = depth // 4
    piece = jax.ShapeDtypeStruct((quarter, width), jnp.bfloat16)
    piece_spec = pl.BlockSpec((quarter, tile), lambda t, places: (0, t))
    return pl.pallas_call(
        grads_body,
        out_shape=(piece,) * 4 + (jax.ShapeDtypeStruct((crops, depth), jnp.float32),),
        grid_spec=pltpu.PrefetchScalarGridSpec(
            num_scalar_prefetch=1,
            grid=(count,),
            in_specs=[
                whole((crops, depth)),
                whole((crops, depth)),
                whole((depth, crops)),
                pl.BlockSpec(
                    (depth, tile),
                    lambda t, places: (0, places[1] * tiles + begin + t),
                ),
                pl.BlockSpec((depth, tile), lambda t, places: (0, t)),
                whole((crops, 128)),
                whole((crops, 128)),
                pl.BlockSpec((1, tile), lambda t, places: (0, begin + t)),
                whole((crops, depth)),
            ],
            out_specs=[piece_spec] * 4 + [whole((crops, depth))],
            scratch_shapes=[pltpu.VMEM((crops, tile), jnp.bfloat16)],
        ),
        cost_estimate=cost(
            8 * crops * depth * width, 6 * depth * width + 8 * crops * depth, 2 * crops * width
        ),
        name="gradients",
    )(
        places,
        *embeds,
        turned,
        own,
        arrived,
        *scales,
        column_scale,
        embed_start,
    )


def place_body(places, *refs):
    pieces, after = refs[:4], refs[-1]
    width = after.shape[1]
    step = pl.program_id(1)
    for place, piece in enumerate(pieces):

        @pl.when(pl.program_id(0) == place)
        def _(piece=piece):
            after[...] = piece[:, pl.ds(pl.multiple_of(step * width, width), width)]


def placed_pieces(places, chunk, pieces, before, block_width):
    rows, width = pieces[0].shape
    tile = tile_width(block_width // 4)
    tiles = block_width // 4 // tile
    begin, count = chunk_tiles(block_width // 4)[chunk]
    group = math.gcd(math.gcd(begin, count), tiles)
    operands = [places, *pieces] + ([] if before is None else [before])
    specs = [pl.BlockSpec(memory_space=pltpu.VMEM)] * 4
    if before is not None:
        specs = specs + [pl.BlockSpec(memory_space=pl.ANY)]
    return pl.pallas_call(
        place_body,
        out_shape=jax.ShapeDtypeStruct((rows, block_width), pieces[0].dtype),
        grid_spec=pltpu.PrefetchScalarGridSpec(
            num_scalar_prefetch=1,
            grid=(4, count // group),
            in_specs=specs,
            out_specs=pl.BlockSpec(
                (rows, group * tile),
                lambda p, t, places: (0, (places[4 + p] * tiles + begin) // group + t),
            ),
        ),
        input_output_aliases={} if before is None else {5: 0},
        cost_estimate=cost(0, 16 * rows * width, 0),
        name="placed_pieces",
    )(*operands)


def swapped(value, *axes):
    if axes == ("role", "crop"):
        return lax.ppermute(value, axes, [(0, 3), (1, 2), (2, 1), (3, 0)])
    return lax.ppermute(value, axes[0], [(0, 1), (1, 0)])


def summands(value):
    axes = ("proto", "crop")
    count = lax.axis_size("proto") * lax.axis_size("crop")
    if count & (count - 1):
        return [lax.psum(value, axes)]
    parts = [value]
    stride = 1
    while stride < count:
        if stride > 1:
            parts = [functools.reduce(jnp.add, parts)]
        masks = [stride * k for k in (1, 2, 3) if stride * k < count]
        for mask in masks:
            pairs = [(place, place ^ mask) for place in range(count)]
            parts.append(lax.ppermute(parts[0], axes, pairs))
        stride *= 4
    return parts


def halving_masks(axis):
    count = lax.axis_size(axis)
    return [1 << bit for bit in range(count.bit_length() - 1)]


def is_power_of_two(count):
    return count & (count - 1) == 0


def flipped(value, axis, mask):
    return lax.ppermute(value, axis, [(p, p ^ mask) for p in range(lax.axis_size(axis))])


def bit_of(place, mask):
    return jnp.where((place & mask) != 0, 1, 0)


def scattered(value):
    count = lax.axis_size("proto")
    if not is_power_of_two(count):
        return lax.psum_scatter(value, ("crop", "proto"), scatter_dimension=0, tiled=True)
    width = value.shape[1]
    rows = value.shape[0] // 2 // count
    steps = [("crop", 1)] + [("proto", mask) for mask in halving_masks("proto")]
    for axis, mask in steps:
        bit = bit_of(lax.axis_index(axis), mask)
        low = value.shape[0] // 2 if axis == "crop" else rows
        halves = value.reshape(-1, 2, low, width)
        theirs = lax.dynamic_index_in_dim(halves, 1 - bit, 1, keepdims=False)
        mine = lax.dynamic_index_in_dim(halves, bit, 1, keepdims=False)
        got = flipped(theirs.reshape(-1, width), axis, mask)
        value = mine.reshape(-1, width) + got
    return value


def joined(mine, other, bit):
    return jnp.concatenate(
        [jnp.where(bit == 0, mine, other), jnp.where(bit == 0, other, mine)], axis=0
    )


def step(embeddings, weights):
    role_place = lax.axis_index("role")
    crop_place = lax.axis_index("crop")
    own_embed = embeddings[0]
    own_weight = weights[0]
    crops = 2 * own_embed.shape[0]
    depth = own_embed.shape[1]
    block_width = own_weight.shape[1]
    teaches = role_place == 0

    own_quarter = 2 * crop_place + role_place
    partner_quarter = 2 * crop_place + 1 - role_place
    order = [own_quarter, own_quarter ^ 2, own_quarter ^ 1, own_quarter ^ 3]
    places = jnp.stack([role_place, own_quarter, partner_quarter, crop_place] + order).astype(
        jnp.int32
    )

    first_columns = columns_of(places, own_weight, 0)
    arrived = [swapped(first_columns, "role")]
    crop_embed = swapped(own_embed, "crop")
    proto_place = lax.axis_index("proto")
    spread = is_power_of_two(lax.axis_size("proto"))
    masks = halving_masks("proto") if spread else []
    part_rows = own_embed.shape[0] // lax.axis_size("proto") if spread else own_embed.shape[0]
    part_start = part_rows * proto_place if spread else 0
    role_embed = swapped(lax.dynamic_slice_in_dim(own_embed, part_start, part_rows), "role")
    got_embed = None
    if masks:
        got_embed = flipped(role_embed, "proto", masks[0])
    own_all = joined(own_embed, crop_embed, crop_place)

    scale = jnp.where(teaches, LOG2E / 0.07, LOG2E / 0.1).astype(jnp.float32).reshape(1)
    parts = []
    for iteration in range(ITERS):
        row_sums, own_factor, partner_factor, *columns = sinkhorn_pass(
            places, scale, own_all, own_weight, parts
        )
        if iteration == 0:
            for chunk in range(1, CHUNKS):
                arrived.append(swapped(columns[chunk - 1], "role"))
        parts = summands(row_sums)
        for place, mask in enumerate(masks):
            if min(place, ITERS - 1) != iteration:
                continue
            role_embed, got_embed, _ = lax.optimization_barrier((role_embed, got_embed, row_sums))
            role_embed = joined(role_embed, got_embed, bit_of(proto_place, mask))
            if place + 1 < len(masks):
                got_embed = flipped(role_embed, "proto", masks[place + 1])

    role_embed, own_all, _ = lax.optimization_barrier((role_embed, own_all, row_sums))
    diagonal_embed = swapped(role_embed, "crop")
    other_all = joined(role_embed, diagonal_embed, crop_place)
    embeds = (jnp.where(teaches, own_all, other_all), jnp.where(teaches, other_all, own_all))
    blocks = embeds[1].T.reshape(4, depth // 4, crops)
    turned = jnp.concatenate(
        [lax.dynamic_index_in_dim(blocks, place, 0, keepdims=False) for place in order], axis=0
    )

    got_factor = swapped(partner_factor, "role")
    inverse = 1.0 / functools.reduce(jnp.add, parts)
    got_inverse = swapped(inverse, "role")
    row_scale, inverse_sum, columns = final_scales(
        places, parts, got_inverse, own_factor, got_factor
    )

    embed_part = jnp.zeros((crops, depth), jnp.float32)
    result = None
    for chunk in GRAD_ORDER:
        kept_piece, crop_piece, role_piece, diagonal_piece, embed_part = gradients(
            places,
            chunk,
            embeds,
            turned,
            own_weight,
            arrived[chunk],
            (row_scale, inverse_sum),
            columns,
            embed_part,
        )
        diagonal_piece = swapped(diagonal_piece, "role", "crop")
        role_piece = swapped(role_piece, "role")
        crop_piece = swapped(crop_piece, "crop")
        pieces = (kept_piece, crop_piece, role_piece, diagonal_piece)
        result = placed_pieces(places, chunk, pieces, result, block_width)
    weight_block = result.reshape(1, 1, depth // 4, block_width)

    summed = scattered(embed_part)
    sides = summed.reshape(summed.shape[0], 2, depth // 2)
    theirs = lax.dynamic_index_in_dim(sides, 1 - role_place, 1, keepdims=False)
    mine = lax.dynamic_index_in_dim(sides, role_place, 1, keepdims=False)
    got_side = swapped(theirs, "role")
    embed_block = (mine + got_side).astype(jnp.bfloat16)[None]
    return (weight_block, embed_block)


def solution(mesh):
    placed = (P("role", "crop", None), P("role", None, "proto"))
    return jax.shard_map(
        step,
        mesh=mesh,
        in_specs=placed,
        out_specs=(P("crop", "role", None, "proto"), P("crop", "proto", "role")),
        check_vma=False,
    )
```

```python
import functools

import jax
import jax.numpy as jnp
from jax import lax
from jax.experimental import pallas as pl
from jax.experimental.pallas import tpu as pltpu
from jax.sharding import PartitionSpec as P


ITERS = 3
LOG2E = 1.4426950408889634
SHARES = (1, 5, 2, 4, 4)
CHUNKS = len(SHARES)
SLICED = 2
GRAD_ORDER = (2, 1, 3, 4, 0)
ROWS = 256
LINES = 16
NT = (((1,), (1,)), ((), ()))


def whole(shape):
    return pl.BlockSpec(shape, lambda *_: (0,) * len(shape), pipeline_mode=pl.Buffered(1))


def cost(flops, bytes_accessed, transcendentals):
    return pl.CostEstimate(
        flops=flops, bytes_accessed=bytes_accessed, transcendentals=transcendentals
    )


def tile_width(quarter_width):
    return 512 if quarter_width % 8192 == 0 else 128


def chunk_tiles(quarter_width):
    tiles = quarter_width // tile_width(quarter_width)
    if tiles % sum(SHARES) == 0:
        counts = [tiles * share // sum(SHARES) for share in SHARES]
    else:
        pairs, rest = divmod(tiles // 2 - 1, CHUNKS - SLICED)
        counts = [1] * SLICED + [2 * (pairs + (n < rest)) for n in range(CHUNKS - SLICED)]
    return [(sum(counts[:n]), count) for n, count in enumerate(counts)]


def pass_tiles(quarter_width):
    tile = 2 * tile_width(quarter_width)
    return tile, quarter_width // tile


def pass_chunks(quarter_width):
    return [(begin // 2, count // 2) for begin, count in chunk_tiles(quarter_width)[SLICED:]]


def lane_tiles(value, width):
    return jnp.concatenate([value] * (width // value.shape[1]), axis=1)


def columns_body(tile, begin, places, matrix, target, arrived):
    width = target.shape[1]
    start = pl.multiple_of(places[2] * (matrix.shape[1] // 4) + begin * tile, tile)
    copy = pltpu.make_async_copy(matrix.at[:, pl.ds(start, width)], target, arrived)
    copy.start()
    copy.wait()


def columns_of(places, matrix, chunk):
    depth = matrix.shape[0]
    quarter_width = matrix.shape[1] // 4
    tile = tile_width(quarter_width)
    begin, count = chunk_tiles(quarter_width)[chunk]
    width = count * tile
    return pl.pallas_call(
        functools.partial(columns_body, tile, begin),
        out_shape=jax.ShapeDtypeStruct((depth, width), matrix.dtype),
        grid_spec=pltpu.PrefetchScalarGridSpec(
            num_scalar_prefetch=1,
            grid=(1,),
            in_specs=[pl.BlockSpec(memory_space=pl.ANY)],
            out_specs=pl.BlockSpec(memory_space=pltpu.VMEM),
            scratch_shapes=[pltpu.SemaphoreType.DMA],
        ),
        cost_estimate=cost(0, 4 * depth * width, 0),
        name="columns_of",
    )(places, matrix)


def reciprocal_rows(parts, crops):
    total = parts[0][...]
    for part in parts[1:]:
        total = total + part[...]
    return jnp.transpose(jnp.broadcast_to(1.0 / total, (128, crops)))


def folded(value):
    total = value[:, :128]
    for lane in range(128, value.shape[1], 128):
        total += value[:, lane : lane + 128]
    return total


def finish_tile(places, tiles, step, total, powers, own_factor, partner_factor, sums):
    factor = jnp.where(
        places[0] == 1, 1.0, 1.0 / jnp.sum(total, axis=0, keepdims=True)
    )
    owned = step // tiles == places[0]

    @pl.when(owned)
    def _():
        own_factor[...] = factor

    @pl.when(jnp.logical_not(owned))
    def _():
        partner_factor[...] = factor

    for start in range(0, powers.shape[0], LINES):
        rows = pl.ds(start, LINES)
        sums[rows, :] += folded(powers[rows, :] * factor)


def finish_pass(row_sums, sums):
    @pl.when(pl.program_id(0) == pl.num_programs(0) - 1)
    def _():
        row_sums[...] = lax.dot_general(
            jnp.ones((8, 128), jnp.float32),
            sums[...],
            NT,
            precision=lax.Precision.HIGHEST,
            preferred_element_type=jnp.float32,
        )[:1]


def first_body(tiles, places, scale, embed, weight, *refs):
    row_sums, own_factor, partner_factor, powers = refs[:4]
    sent, sums = refs[4:-1], refs[-1]
    step = pl.program_id(0)
    crops = embed.shape[0]
    width = weight.shape[1]

    @pl.when(step == 0)
    def _():
        sums[...] = jnp.zeros_like(sums)

    block = weight[...]
    total = jnp.zeros((8, width), jnp.float32)
    for start in range(0, crops, ROWS):
        rows = pl.ds(start, ROWS)
        scores = jnp.dot(embed[rows, :], block, preferred_element_type=jnp.float32)
        part = jnp.exp2(scores * scale[0])
        powers[rows, :] = part
        total += jnp.sum(part.reshape(ROWS // 8, 8, width), axis=0)
    foreign = step // tiles != places[0]
    here = lax.rem(step, tiles)
    for (begin, count), piece in zip(pass_chunks(tiles * width), sent):

        @pl.when(foreign & (here >= begin) & (here < begin + count))
        def _(piece=piece):
            piece[...] = block

    finish_tile(places, tiles, step, total, powers, own_factor, partner_factor, sums)
    finish_pass(row_sums, sums)


def later_body(nparts, tiles, places, powers, *refs):
    parts, refs = refs[:nparts], refs[nparts:]
    row_sums, own_factor, partner_factor, sums, row_scale = refs
    group, crops, width = powers.shape

    @pl.when(pl.program_id(0) == 0)
    def _():
        sums[...] = jnp.zeros_like(sums)
        row_scale[...] = reciprocal_rows(parts, crops)

    for place in range(group):
        tile = powers.at[place]
        lanes = pl.ds(place * width, width)
        total = jnp.zeros((8, width), jnp.float32)
        for start in range(0, crops, 8):
            rows = pl.ds(start, 8)
            total += tile[rows, :] * lane_tiles(row_scale[rows, :], width)
        finish_tile(
            places,
            tiles,
            pl.program_id(0) * group,
            total,
            tile,
            own_factor.at[:, lanes],
            partner_factor.at[:, lanes],
            sums,
        )
    finish_pass(row_sums, sums)


def pass_outputs(crops, quarter_width, group=1):
    tile, tiles = pass_tiles(quarter_width)
    tile, tiles = tile * group, tiles // group

    def owner_spec(partner):
        def index(t, places):
            begin = tiles * (1 - places[0] if partner else places[0])
            return (0, jnp.clip(t - begin, 0, tiles - 1))

        return pl.BlockSpec((1, tile), index)

    factor_shape = jax.ShapeDtypeStruct((1, quarter_width), jnp.float32)
    shapes = [jax.ShapeDtypeStruct((1, crops), jnp.float32), factor_shape, factor_shape]
    return shapes, [whole((1, crops)), owner_spec(False), owner_spec(True)]


def first_pass(places, scale, embed, weight):
    crops, depth = embed.shape
    quarter_width = weight.shape[1] // 4
    tile, tiles = pass_tiles(quarter_width)
    sent = pass_chunks(quarter_width)
    shapes, specs = pass_outputs(crops, quarter_width)

    def sent_spec(begin, count):
        def index(t, places):
            return (0, jnp.clip(t - tiles * (1 - places[0]) - begin, 0, count - 1))

        return pl.BlockSpec((depth, tile), index)

    return pl.pallas_call(
        functools.partial(first_body, tiles),
        out_shape=shapes
        + [jax.ShapeDtypeStruct((2 * tiles, crops, tile), jnp.float32)]
        + [jax.ShapeDtypeStruct((depth, count * tile), weight.dtype) for _, count in sent],
        grid_spec=pltpu.PrefetchScalarGridSpec(
            num_scalar_prefetch=1,
            grid=(2 * tiles,),
            in_specs=[
                pl.BlockSpec(memory_space=pltpu.SMEM),
                whole((crops, depth)),
                pl.BlockSpec((depth, tile), lambda t, places: (0, places[3] * 2 * tiles + t)),
            ],
            out_specs=specs
            + [pl.BlockSpec((None, crops, tile), lambda t, places: (t, 0, 0))]
            + [sent_spec(begin, count) for begin, count in sent],
            scratch_shapes=[pltpu.VMEM((crops, 128), jnp.float32)],
        ),
        cost_estimate=cost(
            4 * crops * depth * quarter_width,
            4 * depth * quarter_width + 8 * crops * quarter_width,
            2 * crops * quarter_width,
        ),
        name="first_pass",
    )(places, scale, embed, weight)


def later_pass(places, powers, parts):
    tiles, crops, tile = powers.shape[0] // 2, *powers.shape[1:]
    quarter_width = tiles * tile
    group = 2 if tiles % 2 == 0 else 1
    shapes, specs = pass_outputs(crops, quarter_width, group)
    return pl.pallas_call(
        functools.partial(later_body, len(parts), tiles),
        out_shape=shapes,
        grid_spec=pltpu.PrefetchScalarGridSpec(
            num_scalar_prefetch=1,
            grid=(2 * tiles // group,),
            in_specs=[
                pl.BlockSpec((group, crops, tile), lambda t, places: (t, 0, 0)),
                *[pl.BlockSpec(memory_space=pltpu.VMEM) for _ in parts],
            ],
            out_specs=specs,
            scratch_shapes=[
                pltpu.VMEM((crops, 128), jnp.float32),
                pltpu.VMEM((crops, 128), jnp.float32),
            ],
        ),
        cost_estimate=cost(8 * crops * quarter_width, 8 * crops * quarter_width, 0),
        name="later_pass",
    )(places, powers, *parts)


def scales_body(nparts, places, *refs):
    parts, (got_inverse, own_factor, got_factor) = refs[:nparts], refs[nparts : nparts + 3]
    row_scale, inverse_sum, column_scale = refs[-3:]
    crops = got_inverse.shape[1]
    mine = reciprocal_rows(parts, crops)
    theirs = jnp.transpose(jnp.broadcast_to(got_inverse[...], (128, crops)))
    teaches = places[0] == 0
    row_scale[...] = jnp.where(teaches, mine, theirs)
    inverse_sum[...] = jnp.where(teaches, theirs, mine)
    column_scale[...] = jnp.where(teaches, own_factor[...], got_factor[...])


def final_scales(places, parts, got_inverse, own_factor, got_factor, ahead):
    crops = got_inverse.shape[1]
    rows = jax.ShapeDtypeStruct((crops, 128), jnp.float32)
    return pl.pallas_call(
        functools.partial(scales_body, len(parts)),
        out_shape=[rows, rows, jax.ShapeDtypeStruct(own_factor.shape, jnp.float32)],
        grid_spec=pltpu.PrefetchScalarGridSpec(
            num_scalar_prefetch=1,
            grid=(1,),
            in_specs=[pl.BlockSpec(memory_space=pltpu.VMEM)] * (len(parts) + 3)
            + [pl.BlockSpec(memory_space=pl.ANY)] * len(ahead),
            out_specs=[pl.BlockSpec(memory_space=pltpu.VMEM)] * 2 + [whole(own_factor.shape)],
        ),
        cost_estimate=cost(0, 8 * crops * 128, 0),
        name="final_scales",
    )(places, *parts, got_inverse, own_factor, got_factor, *ahead)


def grads_body(first, places, other_embed, turned, own, arrived, powers, *refs):
    row_scale, inverse_sum, column_scale = refs[:3]
    embed_start = None if first else refs[3]
    pieces, embed_total, logit_grads = refs[-6:-2], refs[-2], refs[-1]
    crops, width = powers.shape
    quarter = turned.shape[0] // 4

    @pl.when(pl.program_id(0) == 0)
    def _():
        embed_total[...] = jnp.zeros_like(embed_total) if first else embed_start[...]

    def tile(student, divisor, teaches):
        block = arrived[...]
        student_block = student[...]
        factor = column_scale[...]
        for start in range(0, crops, ROWS):
            rows = pl.ds(start, ROWS)
            scores = jnp.dot(other_embed[rows, :], block, preferred_element_type=jnp.float32)
            computed = jnp.exp2(scores * (LOG2E / divisor))
            read = powers[rows, :]
            teacher, student_powers = (read, computed) if teaches else (computed, read)
            targets = (teacher * factor * lane_tiles(row_scale[rows, :], width)).astype(
                jnp.bfloat16
            )
            probs = student_powers * lane_tiles(inverse_sum[rows, :], width)
            grads = ((probs - targets.astype(jnp.float32)) * 10.0).astype(jnp.bfloat16)
            logit_grads[rows, :] = grads
            embed_total[rows, :] += lax.dot_general(
                grads, student_block, NT, preferred_element_type=jnp.float32
            )
        for place, piece in enumerate(pieces):
            piece[...] = jnp.dot(
                turned[pl.ds(place * quarter, quarter), :],
                logit_grads[...],
                preferred_element_type=jnp.float32,
            ).astype(piece.dtype)

    @pl.when(places[0] == 0)
    def _():
        tile(arrived, 0.1, True)

    @pl.when(places[0] == 1)
    def _():
        tile(own, 0.07, False)


def gradients(
    places, chunk, other_embed, turned, own, arrived, powers, scales, column_scale, embed_start
):
    crops, depth = other_embed.shape
    width = arrived.shape[1]
    quarter_width = own.shape[1] // 4
    tile = tile_width(quarter_width)
    tiles = quarter_width // tile
    begin, count = chunk_tiles(quarter_width)[chunk]
    quarter = depth // 4
    piece = jax.ShapeDtypeStruct((quarter, width), jnp.bfloat16)
    piece_spec = pl.BlockSpec((quarter, tile), lambda t, places: (0, t))
    starts = [] if embed_start is None else [embed_start]
    resident = pl.BlockSpec(memory_space=pltpu.VMEM)
    return pl.pallas_call(
        functools.partial(grads_body, embed_start is None),
        out_shape=(piece,) * 4 + (jax.ShapeDtypeStruct((crops, depth), jnp.float32),),
        grid_spec=pltpu.PrefetchScalarGridSpec(
            num_scalar_prefetch=1,
            grid=(count,),
            in_specs=[
                resident,
                resident,
                pl.BlockSpec((depth, tile), lambda t, places: (0, places[1] * tiles + begin + t)),
                pl.BlockSpec((depth, tile), lambda t, places: (0, t)),
                pl.BlockSpec(
                    (None, crops, tile),
                    lambda t, places: (
                        (places[0] * tiles + begin + t) // 2,
                        0,
                        lax.rem(begin + t, 2),
                    ),
                ),
                resident,
                resident,
                pl.BlockSpec((1, tile), lambda t, places: (0, begin + t)),
                *[resident for _ in starts],
            ],
            out_specs=[piece_spec] * 4 + [resident],
            scratch_shapes=[pltpu.VMEM((crops, tile), jnp.bfloat16)],
        ),
        cost_estimate=cost(
            6 * crops * depth * width,
            6 * depth * width + 4 * crops * width + 8 * crops * depth,
            crops * width,
        ),
        name="gradients",
    )(places, other_embed, turned, own, arrived, powers, *scales, column_scale, *starts)


def place_body(tiles, begin, tile, places, *refs):
    pieces, after, arrivals = refs[:4], refs[-2], refs[-1]
    width = pieces[0].shape[1]
    copies = []
    for place, piece in enumerate(pieces):
        start = pl.multiple_of((places[4 + place] * tiles + begin) * tile, tile)
        copies.append(
            pltpu.make_async_copy(piece, after.at[:, pl.ds(start, width)], arrivals.at[place])
        )
    for copy in copies:
        copy.start()
    for copy in copies:
        copy.wait()


def placed_pieces(places, chunk, pieces, before, block_width):
    rows, width = pieces[0].shape
    tile = tile_width(block_width // 4)
    tiles = block_width // 4 // tile
    begin, _ = chunk_tiles(block_width // 4)[chunk]
    operands = [places, *pieces] + ([] if before is None else [before])
    specs = [pl.BlockSpec(memory_space=pltpu.VMEM)] * 4
    if before is not None:
        specs = specs + [pl.BlockSpec(memory_space=pl.ANY)]
    return pl.pallas_call(
        functools.partial(place_body, tiles, begin, tile),
        out_shape=jax.ShapeDtypeStruct((rows, block_width), pieces[0].dtype),
        grid_spec=pltpu.PrefetchScalarGridSpec(
            num_scalar_prefetch=1,
            grid=(1,),
            in_specs=specs,
            out_specs=pl.BlockSpec(memory_space=pl.ANY),
            scratch_shapes=[pltpu.SemaphoreType.DMA((4,))],
        ),
        input_output_aliases={} if before is None else {5: 0},
        cost_estimate=cost(0, 16 * rows * width, 0),
        name="placed_pieces",
    )(*operands)


def swapped(value, *axes):
    if axes == ("role", "crop"):
        return lax.ppermute(value, axes, [(0, 3), (1, 2), (2, 1), (3, 0)])
    return lax.ppermute(value, axes[0], [(0, 1), (1, 0)])


def summands(value):
    axes = ("proto", "crop")
    count = lax.axis_size("proto") * lax.axis_size("crop")
    if count & (count - 1):
        return [lax.psum(value, axes)]
    parts = [value]
    stride = 1
    while stride < count:
        if stride > 1:
            parts = [functools.reduce(jnp.add, parts)]
        masks = [stride * k for k in (1, 2, 3) if stride * k < count]
        for mask in masks:
            pairs = [(place, place ^ mask) for place in range(count)]
            parts.append(lax.ppermute(parts[0], axes, pairs))
        stride *= 4
    return parts


def halving_masks(axis):
    count = lax.axis_size(axis)
    return [1 << bit for bit in range(count.bit_length() - 1)]


def is_power_of_two(count):
    return count & (count - 1) == 0


def flipped(value, axis, mask):
    return lax.ppermute(value, axis, [(p, p ^ mask) for p in range(lax.axis_size(axis))])


def bit_of(place, mask):
    return jnp.where((place & mask) != 0, 1, 0)


def scattered(value):
    count = lax.axis_size("proto")
    if not is_power_of_two(count):
        return lax.psum_scatter(value, ("crop", "proto"), scatter_dimension=0, tiled=True)
    width = value.shape[1]
    rows = value.shape[0] // 2 // count
    steps = [("crop", 1)] + [("proto", mask) for mask in halving_masks("proto")]
    for axis, mask in steps:
        bit = bit_of(lax.axis_index(axis), mask)
        low = value.shape[0] // 2 if axis == "crop" else rows
        halves = value.reshape(-1, 2, low, width)
        theirs = lax.dynamic_index_in_dim(halves, 1 - bit, 1, keepdims=False)
        mine = lax.dynamic_index_in_dim(halves, bit, 1, keepdims=False)
        got = flipped(theirs.reshape(-1, width), axis, mask)
        value = mine.reshape(-1, width) + got
    return value


def joined(mine, other, bit):
    return jnp.concatenate(
        [jnp.where(bit == 0, mine, other), jnp.where(bit == 0, other, mine)], axis=0
    )


def step(embeddings, weights):
    role_place = lax.axis_index("role")
    crop_place = lax.axis_index("crop")
    own_embed = embeddings[0]
    own_weight = weights[0]
    crops = 2 * own_embed.shape[0]
    depth = own_embed.shape[1]
    block_width = own_weight.shape[1]
    teaches = role_place == 0

    own_quarter = 2 * crop_place + role_place
    partner_quarter = 2 * crop_place + 1 - role_place
    order = [own_quarter, own_quarter ^ 2, own_quarter ^ 1, own_quarter ^ 3]
    places = jnp.stack([role_place, own_quarter, partner_quarter, crop_place] + order).astype(
        jnp.int32
    )

    crop_embed = swapped(own_embed, "crop")
    arrived = []
    for chunk in range(SLICED):
        sent = columns_of(places, own_weight, chunk)
        arrived.append(swapped(sent, "role"))
    proto_place = lax.axis_index("proto")
    spread = is_power_of_two(lax.axis_size("proto"))
    masks = halving_masks("proto") if spread else []
    part_rows = own_embed.shape[0] // lax.axis_size("proto") if spread else own_embed.shape[0]
    part_start = part_rows * proto_place if spread else 0
    role_embed = swapped(lax.dynamic_slice_in_dim(own_embed, part_start, part_rows), "role")
    got_embed = None
    if masks:
        got_embed = flipped(role_embed, "proto", masks[0])
    own_all = joined(own_embed, crop_embed, crop_place)

    scale = jnp.where(teaches, LOG2E / 0.07, LOG2E / 0.1).astype(jnp.float32).reshape(1)
    parts = []
    diagonal_embed = None
    for iteration in range(ITERS):
        if iteration == 0:
            row_sums, own_factor, partner_factor, powers, *columns = first_pass(
                places, scale, own_all, own_weight
            )
        else:
            row_sums, own_factor, partner_factor = later_pass(places, powers, parts)
        if iteration == 0:
            for chunk in range(SLICED, CHUNKS):
                arrived.append(swapped(columns[chunk - SLICED], "role"))
        parts = summands(row_sums)
        for place, mask in enumerate(masks):
            if min(place, ITERS - 1) != iteration:
                continue
            role_embed, got_embed, _ = lax.optimization_barrier((role_embed, got_embed, row_sums))
            role_embed = joined(role_embed, got_embed, bit_of(proto_place, mask))
            if place + 1 < len(masks):
                got_embed = flipped(role_embed, "proto", masks[place + 1])

        if iteration == ITERS - 1:
            diagonal_embed = swapped(role_embed, "crop")
    role_embed, diagonal_embed, own_all, _ = lax.optimization_barrier(
        (role_embed, diagonal_embed, own_all, row_sums)
    )
    other_all = joined(role_embed, diagonal_embed, crop_place)
    blocks = jnp.where(teaches, other_all, own_all).T.reshape(4, depth // 4, crops)
    turned = jnp.concatenate(
        [lax.dynamic_index_in_dim(blocks, place, 0, keepdims=False) for place in order], axis=0
    )

    got_factor = swapped(partner_factor, "role")
    inverse = 1.0 / functools.reduce(jnp.add, parts)
    got_inverse = swapped(inverse, "role")
    row_scale, inverse_sum, columns = final_scales(
        places, parts, got_inverse, own_factor, got_factor, (turned, other_all)
    )

    embed_part = None
    result = None
    for chunk in GRAD_ORDER:
        kept_piece, crop_piece, role_piece, diagonal_piece, embed_part = gradients(
            places,
            chunk,
            other_all,
            turned,
            own_weight,
            arrived[chunk],
            powers,
            (row_scale, inverse_sum),
            columns,
            embed_part,
        )
        diagonal_piece = swapped(diagonal_piece, "role", "crop")
        role_piece = swapped(role_piece, "role")
        crop_piece = swapped(crop_piece, "crop")
        pieces = (kept_piece, crop_piece, role_piece, diagonal_piece)
        result = placed_pieces(places, chunk, pieces, result, block_width)
    weight_block = result.reshape(1, 1, depth // 4, block_width)

    summed = scattered(embed_part)
    sides = summed.reshape(summed.shape[0], 2, depth // 2)
    theirs = lax.dynamic_index_in_dim(sides, 1 - role_place, 1, keepdims=False)
    mine = lax.dynamic_index_in_dim(sides, role_place, 1, keepdims=False)
    got_side = swapped(theirs, "role")
    embed_block = (mine + got_side).astype(jnp.bfloat16)[None]
    return (weight_block, embed_block)


def solution(mesh):
    placed = (P("role", "crop", None), P("role", None, "proto"))
    return jax.shard_map(
        step,
        mesh=mesh,
        in_specs=placed,
        out_specs=(P("crop", "role", None, "proto"), P("crop", "proto", "role")),
        check_vma=False,
    )
```

```python
import functools

import jax
import jax.numpy as jnp
from jax import lax
from jax.experimental import pallas as pl
from jax.experimental.pallas import tpu as pltpu
from jax.sharding import PartitionSpec as P


ITERS = 3
LOG2E = 1.4426950408889634
SHARES = (1, 5, 2, 4, 4)
CHUNKS = len(SHARES)
SLICED = 2
GRAD_ORDER = (2, 1, 3, 4, 0)
ROWS = 256
LINES = 16
NT = (((1,), (1,)), ((), ()))


def whole(shape):
    return pl.BlockSpec(shape, lambda *_: (0,) * len(shape), pipeline_mode=pl.Buffered(1))


def cost(flops, bytes_accessed, transcendentals):
    return pl.CostEstimate(
        flops=flops, bytes_accessed=bytes_accessed, transcendentals=transcendentals
    )


def tile_width(quarter_width):
    return 512 if quarter_width % 8192 == 0 else 128


def chunk_tiles(quarter_width):
    tiles = quarter_width // tile_width(quarter_width)
    if tiles % sum(SHARES) == 0:
        counts = [tiles * share // sum(SHARES) for share in SHARES]
    else:
        pairs, rest = divmod(tiles // 2 - 1, CHUNKS - SLICED)
        counts = [1] * SLICED + [2 * (pairs + (n < rest)) for n in range(CHUNKS - SLICED)]
    return [(sum(counts[:n]), count) for n, count in enumerate(counts)]


def pass_tiles(quarter_width):
    tile = 2 * tile_width(quarter_width)
    return tile, quarter_width // tile


def pass_chunks(quarter_width):
    return [(begin // 2, count // 2) for begin, count in chunk_tiles(quarter_width)[SLICED:]]


def lane_tiles(value, width):
    return jnp.concatenate([value] * (width // value.shape[1]), axis=1)


def quarter_of(role_place, crop_place):
    return 2 * crop_place + role_place


def columns_body(tile, begin, matrix, target, arrived):
    width = target.shape[1]
    partner = quarter_of(1 - lax.axis_index("role"), lax.axis_index("crop"))
    start = pl.multiple_of(partner * (matrix.shape[1] // 4) + begin * tile, tile)
    copy = pltpu.make_async_copy(matrix.at[:, pl.ds(start, width)], target, arrived)
    copy.start()
    copy.wait()


def columns_of(matrix, chunk):
    depth = matrix.shape[0]
    quarter_width = matrix.shape[1] // 4
    tile = tile_width(quarter_width)
    begin, count = chunk_tiles(quarter_width)[chunk]
    width = count * tile
    return pl.pallas_call(
        functools.partial(columns_body, tile, begin),
        out_shape=jax.ShapeDtypeStruct((depth, width), matrix.dtype),
        in_specs=[pl.BlockSpec(memory_space=pl.ANY)],
        out_specs=pl.BlockSpec(memory_space=pltpu.VMEM),
        scratch_shapes=[pltpu.SemaphoreType.DMA],
        cost_estimate=cost(0, 4 * depth * width, 0),
        name="columns_of",
    )(matrix)


def reciprocal_rows(parts, crops):
    total = parts[0][...]
    for part in parts[1:]:
        total = total + part[...]
    return jnp.transpose(jnp.broadcast_to(1.0 / total, (128, crops)))


def folded(value):
    total = value[:, :128]
    for lane in range(128, value.shape[1], 128):
        total += value[:, lane : lane + 128]
    return total


def finish_tile(places, tiles, step, total, powers, own_factor, partner_factor, sums):
    factor = jnp.where(
        places[0] == 1, 1.0, 1.0 / jnp.sum(total, axis=0, keepdims=True)
    )
    owned = step // tiles == places[0]

    @pl.when(owned)
    def _():
        own_factor[...] = factor

    @pl.when(jnp.logical_not(owned))
    def _():
        partner_factor[...] = factor

    for start in range(0, powers.shape[0], LINES):
        rows = pl.ds(start, LINES)
        sums[rows, :] += folded(powers[rows, :] * factor)


def finish_pass(row_sums, sums):
    @pl.when(pl.program_id(0) == pl.num_programs(0) - 1)
    def _():
        row_sums[...] = lax.dot_general(
            jnp.ones((8, 128), jnp.float32),
            sums[...],
            NT,
            precision=lax.Precision.HIGHEST,
            preferred_element_type=jnp.float32,
        )[:1]


def first_body(tiles, places, scale, embed, weight, *refs):
    row_sums, own_factor, partner_factor, powers = refs[:4]
    sent, sums = refs[4:-1], refs[-1]
    step = pl.program_id(0)
    crops = embed.shape[0]
    width = weight.shape[1]

    @pl.when(step == 0)
    def _():
        sums[...] = jnp.zeros_like(sums)

    block = weight[...]
    total = jnp.zeros((8, width), jnp.float32)
    for start in range(0, crops, ROWS):
        rows = pl.ds(start, ROWS)
        scores = jnp.dot(embed[rows, :], block, preferred_element_type=jnp.float32)
        part = jnp.exp2(scores * scale[0])
        powers[rows, :] = part
        total += jnp.sum(part.reshape(ROWS // 8, 8, width), axis=0)
    foreign = step // tiles != places[0]
    here = lax.rem(step, tiles)
    for (begin, count), piece in zip(pass_chunks(tiles * width), sent):

        @pl.when(foreign & (here >= begin) & (here < begin + count))
        def _(piece=piece):
            piece[...] = block

    finish_tile(places, tiles, step, total, powers, own_factor, partner_factor, sums)
    finish_pass(row_sums, sums)


def later_body(nparts, tiles, places, powers, *refs):
    parts, refs = refs[:nparts], refs[nparts:]
    row_sums, own_factor, partner_factor, sums, row_scale = refs
    group, crops, width = powers.shape

    @pl.when(pl.program_id(0) == 0)
    def _():
        sums[...] = jnp.zeros_like(sums)
        row_scale[...] = reciprocal_rows(parts, crops)

    for place in range(group):
        tile = powers.at[place]
        lanes = pl.ds(place * width, width)
        total = jnp.zeros((8, width), jnp.float32)
        for start in range(0, crops, 8):
            rows = pl.ds(start, 8)
            total += tile[rows, :] * lane_tiles(row_scale[rows, :], width)
        finish_tile(
            places,
            tiles,
            pl.program_id(0) * group,
            total,
            tile,
            own_factor.at[:, lanes],
            partner_factor.at[:, lanes],
            sums,
        )
    finish_pass(row_sums, sums)


def pass_outputs(crops, quarter_width, group=1):
    tile, tiles = pass_tiles(quarter_width)
    tile, tiles = tile * group, tiles // group

    def owner_spec(partner):
        def index(t, places):
            begin = tiles * (1 - places[0] if partner else places[0])
            return (0, jnp.clip(t - begin, 0, tiles - 1))

        return pl.BlockSpec((1, tile), index)

    factor_shape = jax.ShapeDtypeStruct((1, quarter_width), jnp.float32)
    shapes = [jax.ShapeDtypeStruct((1, crops), jnp.float32), factor_shape, factor_shape]
    return shapes, [whole((1, crops)), owner_spec(False), owner_spec(True)]


def first_pass(places, scale, embed, weight):
    crops, depth = embed.shape
    quarter_width = weight.shape[1] // 4
    tile, tiles = pass_tiles(quarter_width)
    sent = pass_chunks(quarter_width)
    shapes, specs = pass_outputs(crops, quarter_width)

    def sent_spec(begin, count):
        def index(t, places):
            return (0, jnp.clip(t - tiles * (1 - places[0]) - begin, 0, count - 1))

        return pl.BlockSpec((depth, tile), index)

    return pl.pallas_call(
        functools.partial(first_body, tiles),
        out_shape=shapes
        + [jax.ShapeDtypeStruct((2 * tiles, crops, tile), jnp.float32)]
        + [jax.ShapeDtypeStruct((depth, count * tile), weight.dtype) for _, count in sent],
        grid_spec=pltpu.PrefetchScalarGridSpec(
            num_scalar_prefetch=1,
            grid=(2 * tiles,),
            in_specs=[
                pl.BlockSpec(memory_space=pltpu.SMEM),
                whole((crops, depth)),
                pl.BlockSpec((depth, tile), lambda t, places: (0, places[3] * 2 * tiles + t)),
            ],
            out_specs=specs
            + [pl.BlockSpec((None, crops, tile), lambda t, places: (t, 0, 0))]
            + [sent_spec(begin, count) for begin, count in sent],
            scratch_shapes=[pltpu.VMEM((crops, 128), jnp.float32)],
        ),
        cost_estimate=cost(
            4 * crops * depth * quarter_width,
            4 * depth * quarter_width + 8 * crops * quarter_width,
            2 * crops * quarter_width,
        ),
        name="first_pass",
    )(places, scale, embed, weight)


def later_pass(places, powers, parts):
    tiles, crops, tile = powers.shape[0] // 2, *powers.shape[1:]
    quarter_width = tiles * tile
    group = 2 if tiles % 2 == 0 else 1
    shapes, specs = pass_outputs(crops, quarter_width, group)
    return pl.pallas_call(
        functools.partial(later_body, len(parts), tiles),
        out_shape=shapes,
        grid_spec=pltpu.PrefetchScalarGridSpec(
            num_scalar_prefetch=1,
            grid=(2 * tiles // group,),
            in_specs=[
                pl.BlockSpec((group, crops, tile), lambda t, places: (t, 0, 0)),
                *[pl.BlockSpec(memory_space=pltpu.VMEM) for _ in parts],
            ],
            out_specs=specs,
            scratch_shapes=[
                pltpu.VMEM((crops, 128), jnp.float32),
                pltpu.VMEM((crops, 128), jnp.float32),
            ],
        ),
        cost_estimate=cost(8 * crops * quarter_width, 8 * crops * quarter_width, 0),
        name="later_pass",
    )(places, powers, *parts)


def scales_body(nparts, places, *refs):
    parts, (got_inverse, own_factor, got_factor) = refs[:nparts], refs[nparts : nparts + 3]
    row_scale, inverse_sum, column_scale = refs[-3:]
    crops = got_inverse.shape[1]
    mine = reciprocal_rows(parts, crops)
    theirs = jnp.transpose(jnp.broadcast_to(got_inverse[...], (128, crops)))
    teaches = places[0] == 0
    row_scale[...] = jnp.where(teaches, mine, theirs)
    inverse_sum[...] = jnp.where(teaches, theirs, mine)
    column_scale[...] = jnp.where(teaches, own_factor[...], got_factor[...])


def final_scales(places, parts, got_inverse, own_factor, got_factor, ahead):
    crops = got_inverse.shape[1]
    rows = jax.ShapeDtypeStruct((crops, 128), jnp.float32)
    return pl.pallas_call(
        functools.partial(scales_body, len(parts)),
        out_shape=[rows, rows, jax.ShapeDtypeStruct(own_factor.shape, jnp.float32)],
        grid_spec=pltpu.PrefetchScalarGridSpec(
            num_scalar_prefetch=1,
            grid=(1,),
            in_specs=[pl.BlockSpec(memory_space=pltpu.VMEM)] * (len(parts) + 3)
            + [pl.BlockSpec(memory_space=pl.ANY)] * len(ahead),
            out_specs=[pl.BlockSpec(memory_space=pltpu.VMEM)] * 2 + [whole(own_factor.shape)],
        ),
        cost_estimate=cost(0, 8 * crops * 128, 0),
        name="final_scales",
    )(places, *parts, got_inverse, own_factor, got_factor, *ahead)


def grads_body(first, places, other_embed, turned, own, arrived, powers, *refs):
    row_scale, inverse_sum, column_scale = refs[:3]
    embed_start = None if first else refs[3]
    pieces, embed_total, logit_grads = refs[-6:-2], refs[-2], refs[-1]
    crops, width = powers.shape
    quarter = turned.shape[0] // 4

    @pl.when(pl.program_id(0) == 0)
    def _():
        embed_total[...] = jnp.zeros_like(embed_total) if first else embed_start[...]

    def tile(student, divisor, teaches):
        block = arrived[...]
        student_block = student[...]
        factor = column_scale[...]
        for start in range(0, crops, ROWS):
            rows = pl.ds(start, ROWS)
            scores = jnp.dot(other_embed[rows, :], block, preferred_element_type=jnp.float32)
            computed = jnp.exp2(scores * (LOG2E / divisor))
            read = powers[rows, :]
            teacher, student_powers = (read, computed) if teaches else (computed, read)
            targets = (teacher * factor * lane_tiles(row_scale[rows, :], width)).astype(
                jnp.bfloat16
            )
            probs = student_powers * lane_tiles(inverse_sum[rows, :], width)
            grads = ((probs - targets.astype(jnp.float32)) * 10.0).astype(jnp.bfloat16)
            logit_grads[rows, :] = grads
            embed_total[rows, :] += lax.dot_general(
                grads, student_block, NT, preferred_element_type=jnp.float32
            )
        for place, piece in enumerate(pieces):
            piece[...] = jnp.dot(
                turned[pl.ds(place * quarter, quarter), :],
                logit_grads[...],
                preferred_element_type=jnp.float32,
            ).astype(piece.dtype)

    @pl.when(places[0] == 0)
    def _():
        tile(arrived, 0.1, True)

    @pl.when(places[0] == 1)
    def _():
        tile(own, 0.07, False)


def gradients(
    places, chunk, other_embed, turned, own, arrived, powers, scales, column_scale, embed_start
):
    crops, depth = other_embed.shape
    width = arrived.shape[1]
    quarter_width = own.shape[1] // 4
    tile = tile_width(quarter_width)
    tiles = quarter_width // tile
    begin, count = chunk_tiles(quarter_width)[chunk]
    quarter = depth // 4
    piece = jax.ShapeDtypeStruct((quarter, width), jnp.bfloat16)
    piece_spec = pl.BlockSpec((quarter, tile), lambda t, places: (0, t))
    starts = [] if embed_start is None else [embed_start]
    resident = pl.BlockSpec(memory_space=pltpu.VMEM)
    return pl.pallas_call(
        functools.partial(grads_body, embed_start is None),
        out_shape=(piece,) * 4 + (jax.ShapeDtypeStruct((crops, depth), jnp.float32),),
        grid_spec=pltpu.PrefetchScalarGridSpec(
            num_scalar_prefetch=1,
            grid=(count,),
            in_specs=[
                resident,
                resident,
                pl.BlockSpec((depth, tile), lambda t, places: (0, places[1] * tiles + begin + t)),
                pl.BlockSpec((depth, tile), lambda t, places: (0, t)),
                pl.BlockSpec(
                    (None, crops, tile),
                    lambda t, places: (
                        (places[0] * tiles + begin + t) // 2,
                        0,
                        lax.rem(begin + t, 2),
                    ),
                ),
                resident,
                resident,
                pl.BlockSpec((1, tile), lambda t, places: (0, begin + t)),
                *[resident for _ in starts],
            ],
            out_specs=[piece_spec] * 4 + [resident],
            scratch_shapes=[pltpu.VMEM((crops, tile), jnp.bfloat16)],
        ),
        cost_estimate=cost(
            6 * crops * depth * width,
            6 * depth * width + 4 * crops * width + 8 * crops * depth,
            crops * width,
        ),
        name="gradients",
    )(places, other_embed, turned, own, arrived, powers, *scales, column_scale, *starts)


def place_body(tiles, begin, tile, *refs):
    pieces, after, arrivals = refs[:4], refs[-2], refs[-1]
    width = pieces[0].shape[1]
    role_place, crop_place = lax.axis_index("role"), lax.axis_index("crop")
    quarters = [
        quarter_of(role, crop)
        for role in (role_place, 1 - role_place)
        for crop in (crop_place, 1 - crop_place)
    ]
    copies = []
    for place, (quarter, piece) in enumerate(zip(quarters, pieces)):
        start = pl.multiple_of((quarter * tiles + begin) * tile, tile)
        copies.append(
            pltpu.make_async_copy(piece, after.at[:, pl.ds(start, width)], arrivals.at[place])
        )
    for copy in copies:
        copy.start()
    for copy in copies:
        copy.wait()


def placed_pieces(chunk, pieces, before, block_width):
    rows, width = pieces[0].shape
    tile = tile_width(block_width // 4)
    tiles = block_width // 4 // tile
    begin, _ = chunk_tiles(block_width // 4)[chunk]
    operands = [*pieces] + ([] if before is None else [before])
    specs = [pl.BlockSpec(memory_space=pltpu.VMEM)] * 4
    if before is not None:
        specs = specs + [pl.BlockSpec(memory_space=pl.ANY)]
    return pl.pallas_call(
        functools.partial(place_body, tiles, begin, tile),
        out_shape=jax.ShapeDtypeStruct((rows, block_width), pieces[0].dtype),
        in_specs=specs,
        out_specs=pl.BlockSpec(memory_space=pl.ANY),
        scratch_shapes=[pltpu.SemaphoreType.DMA((4,))],
        input_output_aliases={} if before is None else {4: 0},
        cost_estimate=cost(0, 16 * rows * width, 0),
        name="placed_pieces",
    )(*operands)


def swapped(value, *axes):
    if axes == ("role", "crop"):
        return lax.ppermute(value, axes, [(0, 3), (1, 2), (2, 1), (3, 0)])
    return lax.ppermute(value, axes[0], [(0, 1), (1, 0)])


def summands(value):
    axes = ("proto", "crop")
    count = lax.axis_size("proto") * lax.axis_size("crop")
    if count & (count - 1):
        return [lax.psum(value, axes)]
    parts = [value]
    stride = 1
    while stride < count:
        if stride > 1:
            parts = [functools.reduce(jnp.add, parts)]
        masks = [stride * k for k in (1, 2, 3) if stride * k < count]
        for mask in masks:
            pairs = [(place, place ^ mask) for place in range(count)]
            parts.append(lax.ppermute(parts[0], axes, pairs))
        stride *= 4
    return parts


def halving_masks(axis):
    count = lax.axis_size(axis)
    return [1 << bit for bit in range(count.bit_length() - 1)]


def is_power_of_two(count):
    return count & (count - 1) == 0


def flipped(value, axis, mask):
    return lax.ppermute(value, axis, [(p, p ^ mask) for p in range(lax.axis_size(axis))])


def bit_of(place, mask):
    return jnp.where((place & mask) != 0, 1, 0)


def scattered(value):
    count = lax.axis_size("proto")
    if not is_power_of_two(count):
        return lax.psum_scatter(value, ("crop", "proto"), scatter_dimension=0, tiled=True)
    width = value.shape[1]
    rows = value.shape[0] // 2 // count
    steps = [("crop", 1)] + [("proto", mask) for mask in halving_masks("proto")]
    for axis, mask in steps:
        bit = bit_of(lax.axis_index(axis), mask)
        low = value.shape[0] // 2 if axis == "crop" else rows
        halves = value.reshape(-1, 2, low, width)
        theirs = lax.dynamic_index_in_dim(halves, 1 - bit, 1, keepdims=False)
        mine = lax.dynamic_index_in_dim(halves, bit, 1, keepdims=False)
        got = flipped(theirs.reshape(-1, width), axis, mask)
        value = mine.reshape(-1, width) + got
    return value


def joined(mine, other, bit):
    return jnp.concatenate(
        [jnp.where(bit == 0, mine, other), jnp.where(bit == 0, other, mine)], axis=0
    )


def step(embeddings, weights):
    role_place = lax.axis_index("role")
    crop_place = lax.axis_index("crop")
    own_embed = embeddings[0]
    own_weight = weights[0]
    crops = 2 * own_embed.shape[0]
    depth = own_embed.shape[1]
    block_width = own_weight.shape[1]
    teaches = role_place == 0

    own_quarter = quarter_of(role_place, crop_place)
    partner_quarter = quarter_of(1 - role_place, crop_place)
    order = [own_quarter, own_quarter ^ 2, own_quarter ^ 1, own_quarter ^ 3]
    places = jnp.stack([role_place, own_quarter, partner_quarter, crop_place]).astype(jnp.int32)

    crop_embed = swapped(own_embed, "crop")
    arrived = []
    for chunk in range(SLICED):
        sent = columns_of(own_weight, chunk)
        arrived.append(swapped(sent, "role"))
    proto_place = lax.axis_index("proto")
    spread = is_power_of_two(lax.axis_size("proto"))
    masks = halving_masks("proto") if spread else []
    part_rows = own_embed.shape[0] // lax.axis_size("proto") if spread else own_embed.shape[0]
    part_start = part_rows * proto_place if spread else 0
    role_embed = swapped(lax.dynamic_slice_in_dim(own_embed, part_start, part_rows), "role")
    own_all = joined(own_embed, crop_embed, crop_place)

    scale = jnp.where(teaches, LOG2E / 0.07, LOG2E / 0.1).astype(jnp.float32).reshape(1)
    parts = []
    diagonal_embed = None
    for iteration in range(ITERS):
        if iteration == 0:
            row_sums, own_factor, partner_factor, powers, *columns = first_pass(
                places, scale, own_all, own_weight
            )
        else:
            row_sums, own_factor, partner_factor = later_pass(places, powers, parts)
        if iteration == 0:
            for chunk in range(SLICED, CHUNKS):
                arrived.append(swapped(columns[chunk - SLICED], "role"))
        parts = summands(row_sums)
        for place, mask in enumerate(masks):
            if min(max(place - 1, 0), ITERS - 1) != iteration:
                continue
            role_embed, _ = lax.optimization_barrier((role_embed, row_sums))
            got_embed = flipped(role_embed, "proto", mask)
            role_embed = joined(role_embed, got_embed, bit_of(proto_place, mask))

        if iteration == ITERS - 1:
            diagonal_embed = swapped(role_embed, "crop")
    role_embed, diagonal_embed, own_all, _ = lax.optimization_barrier(
        (role_embed, diagonal_embed, own_all, row_sums)
    )
    other_all = joined(role_embed, diagonal_embed, crop_place)
    blocks = jnp.where(teaches, other_all, own_all).T.reshape(4, depth // 4, crops)
    turned = jnp.concatenate(
        [lax.dynamic_index_in_dim(blocks, place, 0, keepdims=False) for place in order], axis=0
    )

    got_factor = swapped(partner_factor, "role")
    inverse = 1.0 / functools.reduce(jnp.add, parts)
    got_inverse = swapped(inverse, "role")
    row_scale, inverse_sum, columns = final_scales(
        places, parts, got_inverse, own_factor, got_factor, (turned, other_all)
    )

    embed_part = None
    result = None
    for chunk in GRAD_ORDER:
        kept_piece, crop_piece, role_piece, diagonal_piece, embed_part = gradients(
            places,
            chunk,
            other_all,
            turned,
            own_weight,
            arrived[chunk],
            powers,
            (row_scale, inverse_sum),
            columns,
            embed_part,
        )
        diagonal_piece = swapped(diagonal_piece, "role", "crop")
        role_piece = swapped(role_piece, "role")
        crop_piece = swapped(crop_piece, "crop")
        pieces = (kept_piece, crop_piece, role_piece, diagonal_piece)
        result = placed_pieces(chunk, pieces, result, block_width)
    weight_block = result.reshape(1, 1, depth // 4, block_width)

    summed = scattered(embed_part)
    sides = summed.reshape(summed.shape[0], 2, depth // 2)
    theirs = lax.dynamic_index_in_dim(sides, 1 - role_place, 1, keepdims=False)
    mine = lax.dynamic_index_in_dim(sides, role_place, 1, keepdims=False)
    got_side = swapped(theirs, "role")
    embed_block = (mine + got_side).astype(jnp.bfloat16)[None]
    return (weight_block, embed_block)


def solution(mesh):
    placed = (P("role", "crop", None), P("role", None, "proto"))
    return jax.shard_map(
        step,
        mesh=mesh,
        in_specs=placed,
        out_specs=(P("crop", "role", None, "proto"), P("crop", "proto", "role")),
        check_vma=False,
    )
```

```python
import functools

import jax
import jax.numpy as jnp
import numpy as np
from jax import lax
from jax.experimental import pallas as pl
from jax.experimental.pallas import tpu as pltpu
from jax.sharding import PartitionSpec as P


ITERS = 3
SHARPEN = float(np.float32(1) / np.float32(0.07))
SOFTEN = float(np.float32(1) / np.float32(0.1))
SHARES = (1, 5, 2, 4, 4)
CHUNKS = len(SHARES)
SLICED = 2
GRAD_ORDER = (2, 1, 3, 4, 0)
ROWS = 256
LINES = 16
NT = (((1,), (1,)), ((), ()))


def whole(shape):
    return pl.BlockSpec(shape, lambda *_: (0,) * len(shape), pipeline_mode=pl.Buffered(1))


def cost(flops, bytes_accessed, transcendentals):
    return pl.CostEstimate(
        flops=flops, bytes_accessed=bytes_accessed, transcendentals=transcendentals
    )


def tile_width(quarter_width):
    return 512 if quarter_width % 8192 == 0 else 128


def chunk_tiles(quarter_width):
    tiles = quarter_width // tile_width(quarter_width)
    if tiles % sum(SHARES) == 0:
        counts = [tiles * share // sum(SHARES) for share in SHARES]
    else:
        pairs, rest = divmod(tiles // 2 - 1, CHUNKS - SLICED)
        counts = [1] * SLICED + [2 * (pairs + (n < rest)) for n in range(CHUNKS - SLICED)]
    return [(sum(counts[:n]), count) for n, count in enumerate(counts)]


def pass_tiles(quarter_width):
    tile = 2 * tile_width(quarter_width)
    return tile, quarter_width // tile


def pass_chunks(quarter_width):
    return [(begin // 2, count // 2) for begin, count in chunk_tiles(quarter_width)[SLICED:]]


def lane_tiles(value, width):
    return jnp.concatenate([value] * (width // value.shape[1]), axis=1)


def quarter_of(role_place, crop_place):
    return 2 * crop_place + role_place


def columns_body(tile, begin, matrix, target, arrived):
    width = target.shape[1]
    partner = quarter_of(1 - lax.axis_index("role"), lax.axis_index("crop"))
    start = pl.multiple_of(partner * (matrix.shape[1] // 4) + begin * tile, tile)
    copy = pltpu.make_async_copy(matrix.at[:, pl.ds(start, width)], target, arrived)
    copy.start()
    copy.wait()


def columns_of(matrix, chunk):
    depth = matrix.shape[0]
    quarter_width = matrix.shape[1] // 4
    tile = tile_width(quarter_width)
    begin, count = chunk_tiles(quarter_width)[chunk]
    width = count * tile
    return pl.pallas_call(
        functools.partial(columns_body, tile, begin),
        out_shape=jax.ShapeDtypeStruct((depth, width), matrix.dtype),
        in_specs=[pl.BlockSpec(memory_space=pl.ANY)],
        out_specs=pl.BlockSpec(memory_space=pltpu.VMEM),
        scratch_shapes=[pltpu.SemaphoreType.DMA],
        cost_estimate=cost(0, 4 * depth * width, 0),
        name="columns_of",
    )(matrix)


def total_of(parts):
    total = parts[0][...]
    for part in parts[1:]:
        total = total + part[...]
    return total


def as_rows(line):
    return jnp.transpose(jnp.broadcast_to(line, (128, line.shape[1])))


def folded(value):
    total = value[:, :128]
    for lane in range(128, value.shape[1], 128):
        total += value[:, lane : lane + 128]
    return total


def finish_tile(places, tiles, step, total, powers, own_factor, partner_factor, sums):
    column_sum = jnp.where(places[0] == 1, 1.0, jnp.sum(total, axis=0, keepdims=True))
    factor = 1.0 / column_sum
    owned = step // tiles == places[0]

    @pl.when(owned)
    def _():
        own_factor[...] = column_sum

    @pl.when(jnp.logical_not(owned))
    def _():
        partner_factor[...] = column_sum

    for start in range(0, powers.shape[0], LINES):
        rows = pl.ds(start, LINES)
        sums[rows, :] += folded(powers[rows, :] * factor)


def finish_pass(row_sums, sums):
    @pl.when(pl.program_id(0) == pl.num_programs(0) - 1)
    def _():
        row_sums[...] = lax.dot_general(
            jnp.ones((8, 128), jnp.float32),
            sums[...],
            NT,
            precision=lax.Precision.HIGHEST,
            preferred_element_type=jnp.float32,
        )[:1]


def first_body(tiles, places, scale, embed, weight, *refs):
    row_sums, own_factor, partner_factor, logits = refs[:4]
    sent, sums, powers = refs[4:-2], refs[-2], refs[-1]
    step = pl.program_id(0)
    crops = embed.shape[0]
    width = weight.shape[1]

    @pl.when(step == 0)
    def _():
        sums[...] = jnp.zeros_like(sums)

    block = weight[...]
    total = jnp.zeros((8, width), jnp.float32)
    for start in range(0, crops, ROWS):
        rows = pl.ds(start, ROWS)
        scores = jnp.dot(embed[rows, :], block, preferred_element_type=jnp.float32)
        scaled = scores * scale[0]
        logits[rows, :] = scaled
        part = jnp.exp(scaled)
        powers[rows, :] = part
        total += jnp.sum(part.reshape(ROWS // 8, 8, width), axis=0)
    foreign = step // tiles != places[0]
    here = lax.rem(step, tiles)
    for (begin, count), piece in zip(pass_chunks(tiles * width), sent):

        @pl.when(foreign & (here >= begin) & (here < begin + count))
        def _(piece=piece):
            piece[...] = block

    finish_tile(places, tiles, step, total, powers, own_factor, partner_factor, sums)
    finish_pass(row_sums, sums)


def later_body(nparts, tiles, places, logits, *refs):
    parts, refs = refs[:nparts], refs[nparts:]
    row_sums, own_factor, partner_factor, sums, row_scale, powers = refs
    group, crops, width = logits.shape

    @pl.when(pl.program_id(0) == 0)
    def _():
        sums[...] = jnp.zeros_like(sums)
        row_scale[...] = as_rows(1.0 / total_of(parts))

    for place in range(group):
        tile = logits.at[place]
        lanes = pl.ds(place * width, width)
        total = jnp.zeros((8, width), jnp.float32)
        for start in range(0, crops, 8):
            rows = pl.ds(start, 8)
            part = jnp.exp(tile[rows, :])
            powers[rows, :] = part
            total += part * lane_tiles(row_scale[rows, :], width)
        finish_tile(
            places,
            tiles,
            pl.program_id(0) * group,
            total,
            powers,
            own_factor.at[:, lanes],
            partner_factor.at[:, lanes],
            sums,
        )
    finish_pass(row_sums, sums)


def pass_outputs(crops, quarter_width, group=1):
    tile, tiles = pass_tiles(quarter_width)
    tile, tiles = tile * group, tiles // group

    def owner_spec(partner):
        def index(t, places):
            begin = tiles * (1 - places[0] if partner else places[0])
            return (0, jnp.clip(t - begin, 0, tiles - 1))

        return pl.BlockSpec((1, tile), index)

    factor_shape = jax.ShapeDtypeStruct((1, quarter_width), jnp.float32)
    shapes = [jax.ShapeDtypeStruct((1, crops), jnp.float32), factor_shape, factor_shape]
    return shapes, [whole((1, crops)), owner_spec(False), owner_spec(True)]


def first_pass(places, scale, embed, weight):
    crops, depth = embed.shape
    quarter_width = weight.shape[1] // 4
    tile, tiles = pass_tiles(quarter_width)
    sent = pass_chunks(quarter_width)
    shapes, specs = pass_outputs(crops, quarter_width)

    def sent_spec(begin, count):
        def index(t, places):
            return (0, jnp.clip(t - tiles * (1 - places[0]) - begin, 0, count - 1))

        return pl.BlockSpec((depth, tile), index)

    return pl.pallas_call(
        functools.partial(first_body, tiles),
        out_shape=shapes
        + [jax.ShapeDtypeStruct((2 * tiles, crops, tile), jnp.float32)]
        + [jax.ShapeDtypeStruct((depth, count * tile), weight.dtype) for _, count in sent],
        grid_spec=pltpu.PrefetchScalarGridSpec(
            num_scalar_prefetch=1,
            grid=(2 * tiles,),
            in_specs=[
                pl.BlockSpec(memory_space=pltpu.SMEM),
                whole((crops, depth)),
                pl.BlockSpec((depth, tile), lambda t, places: (0, places[3] * 2 * tiles + t)),
            ],
            out_specs=specs
            + [pl.BlockSpec((None, crops, tile), lambda t, places: (t, 0, 0))]
            + [sent_spec(begin, count) for begin, count in sent],
            scratch_shapes=[
                pltpu.VMEM((crops, 128), jnp.float32),
                pltpu.VMEM((crops, tile), jnp.float32),
            ],
        ),
        cost_estimate=cost(
            4 * crops * depth * quarter_width,
            4 * depth * quarter_width + 8 * crops * quarter_width,
            2 * crops * quarter_width,
        ),
        name="first_pass",
    )(places, scale, embed, weight)


def later_pass(places, powers, parts):
    tiles, crops, tile = powers.shape[0] // 2, *powers.shape[1:]
    quarter_width = tiles * tile
    group = 2 if tiles % 2 == 0 else 1
    shapes, specs = pass_outputs(crops, quarter_width, group)
    return pl.pallas_call(
        functools.partial(later_body, len(parts), tiles),
        out_shape=shapes,
        grid_spec=pltpu.PrefetchScalarGridSpec(
            num_scalar_prefetch=1,
            grid=(2 * tiles // group,),
            in_specs=[
                pl.BlockSpec((group, crops, tile), lambda t, places: (t, 0, 0)),
                *[pl.BlockSpec(memory_space=pltpu.VMEM) for _ in parts],
            ],
            out_specs=specs,
            scratch_shapes=[
                pltpu.VMEM((crops, 128), jnp.float32),
                pltpu.VMEM((crops, 128), jnp.float32),
                pltpu.VMEM((crops, tile), jnp.float32),
            ],
        ),
        cost_estimate=cost(8 * crops * quarter_width, 8 * crops * quarter_width, 0),
        name="later_pass",
    )(places, powers, *parts)


def scales_body(nparts, places, *refs):
    parts, (got_total, own_sum, got_sum) = refs[:nparts], refs[nparts : nparts + 3]
    row_shift, inverse_sum, column_shift = refs[-3:]
    teaches = places[0] == 0
    mine, theirs = total_of(parts), got_total[...]
    row_shift[...] = as_rows(-jnp.log(jnp.where(teaches, mine, theirs)))
    inverse_sum[...] = as_rows(1.0 / jnp.where(teaches, theirs, mine))
    column_shift[...] = -jnp.log(jnp.where(teaches, own_sum[...], got_sum[...]))


def final_scales(places, parts, got_inverse, own_factor, got_factor, ahead):
    crops = got_inverse.shape[1]
    rows = jax.ShapeDtypeStruct((crops, 128), jnp.float32)
    return pl.pallas_call(
        functools.partial(scales_body, len(parts)),
        out_shape=[rows, rows, jax.ShapeDtypeStruct(own_factor.shape, jnp.float32)],
        grid_spec=pltpu.PrefetchScalarGridSpec(
            num_scalar_prefetch=1,
            grid=(1,),
            in_specs=[pl.BlockSpec(memory_space=pltpu.VMEM)] * (len(parts) + 3)
            + [pl.BlockSpec(memory_space=pl.ANY)] * len(ahead),
            out_specs=[pl.BlockSpec(memory_space=pltpu.VMEM)] * 2 + [whole(own_factor.shape)],
        ),
        cost_estimate=cost(0, 8 * crops * 128, 0),
        name="final_scales",
    )(places, *parts, got_inverse, own_factor, got_factor, *ahead)


def grads_body(first, places, other_embed, turned, own, arrived, powers, *refs):
    row_scale, inverse_sum, column_scale = refs[:3]
    embed_start = None if first else refs[3]
    pieces, embed_total, logit_grads = refs[-6:-2], refs[-2], refs[-1]
    crops, width = powers.shape
    quarter = turned.shape[0] // 4

    @pl.when(pl.program_id(0) == 0)
    def _():
        embed_total[...] = jnp.zeros_like(embed_total) if first else embed_start[...]

    def tile(student, sharpening, teaches):
        block = arrived[...]
        student_block = student[...]
        shift = column_scale[...]
        for start in range(0, crops, ROWS):
            rows = pl.ds(start, ROWS)
            scores = jnp.dot(other_embed[rows, :], block, preferred_element_type=jnp.float32)
            computed = scores * sharpening
            read = powers[rows, :]
            teacher, student_logits = (read, computed) if teaches else (computed, read)
            targets = jnp.exp(
                teacher + shift + lane_tiles(row_scale[rows, :], width)
            ).astype(jnp.bfloat16)
            probs = jnp.exp(student_logits) * lane_tiles(inverse_sum[rows, :], width)
            grads = ((probs - targets.astype(jnp.float32)) * 10.0).astype(jnp.bfloat16)
            logit_grads[rows, :] = grads
            embed_total[rows, :] += lax.dot_general(
                grads, student_block, NT, preferred_element_type=jnp.float32
            )
        for place, piece in enumerate(pieces):
            piece[...] = jnp.dot(
                turned[pl.ds(place * quarter, quarter), :],
                logit_grads[...],
                preferred_element_type=jnp.float32,
            ).astype(piece.dtype)

    @pl.when(places[0] == 0)
    def _():
        tile(arrived, SOFTEN, True)

    @pl.when(places[0] == 1)
    def _():
        tile(own, SHARPEN, False)


def gradients(
    places, chunk, other_embed, turned, own, arrived, powers, scales, column_scale, embed_start
):
    crops, depth = other_embed.shape
    width = arrived.shape[1]
    quarter_width = own.shape[1] // 4
    tile = tile_width(quarter_width)
    tiles = quarter_width // tile
    begin, count = chunk_tiles(quarter_width)[chunk]
    quarter = depth // 4
    piece = jax.ShapeDtypeStruct((quarter, width), jnp.bfloat16)
    piece_spec = pl.BlockSpec((quarter, tile), lambda t, places: (0, t))
    starts = [] if embed_start is None else [embed_start]
    resident = pl.BlockSpec(memory_space=pltpu.VMEM)
    return pl.pallas_call(
        functools.partial(grads_body, embed_start is None),
        out_shape=(piece,) * 4 + (jax.ShapeDtypeStruct((crops, depth), jnp.float32),),
        grid_spec=pltpu.PrefetchScalarGridSpec(
            num_scalar_prefetch=1,
            grid=(count,),
            in_specs=[
                resident,
                resident,
                pl.BlockSpec((depth, tile), lambda t, places: (0, places[1] * tiles + begin + t)),
                pl.BlockSpec((depth, tile), lambda t, places: (0, t)),
                pl.BlockSpec(
                    (None, crops, tile),
                    lambda t, places: (
                        (places[0] * tiles + begin + t) // 2,
                        0,
                        lax.rem(begin + t, 2),
                    ),
                ),
                resident,
                resident,
                pl.BlockSpec((1, tile), lambda t, places: (0, begin + t)),
                *[resident for _ in starts],
            ],
            out_specs=[piece_spec] * 4 + [resident],
            scratch_shapes=[pltpu.VMEM((crops, tile), jnp.bfloat16)],
        ),
        cost_estimate=cost(
            6 * crops * depth * width,
            6 * depth * width + 4 * crops * width + 8 * crops * depth,
            crops * width,
        ),
        name="gradients",
    )(places, other_embed, turned, own, arrived, powers, *scales, column_scale, *starts)


def place_body(tiles, begin, tile, *refs):
    pieces, after, arrivals = refs[:4], refs[-2], refs[-1]
    width = pieces[0].shape[1]
    role_place, crop_place = lax.axis_index("role"), lax.axis_index("crop")
    quarters = [
        quarter_of(role, crop)
        for role in (role_place, 1 - role_place)
        for crop in (crop_place, 1 - crop_place)
    ]
    copies = []
    for place, (quarter, piece) in enumerate(zip(quarters, pieces)):
        start = pl.multiple_of((quarter * tiles + begin) * tile, tile)
        copies.append(
            pltpu.make_async_copy(piece, after.at[:, pl.ds(start, width)], arrivals.at[place])
        )
    for copy in copies:
        copy.start()
    for copy in copies:
        copy.wait()


def placed_pieces(chunk, pieces, before, block_width):
    rows, width = pieces[0].shape
    tile = tile_width(block_width // 4)
    tiles = block_width // 4 // tile
    begin, _ = chunk_tiles(block_width // 4)[chunk]
    operands = [*pieces] + ([] if before is None else [before])
    specs = [pl.BlockSpec(memory_space=pltpu.VMEM)] * 4
    if before is not None:
        specs = specs + [pl.BlockSpec(memory_space=pl.ANY)]
    return pl.pallas_call(
        functools.partial(place_body, tiles, begin, tile),
        out_shape=jax.ShapeDtypeStruct((rows, block_width), pieces[0].dtype),
        in_specs=specs,
        out_specs=pl.BlockSpec(memory_space=pl.ANY),
        scratch_shapes=[pltpu.SemaphoreType.DMA((4,))],
        input_output_aliases={} if before is None else {4: 0},
        cost_estimate=cost(0, 16 * rows * width, 0),
        name="placed_pieces",
    )(*operands)


def swapped(value, *axes):
    if axes == ("role", "crop"):
        return lax.ppermute(value, axes, [(0, 3), (1, 2), (2, 1), (3, 0)])
    return lax.ppermute(value, axes[0], [(0, 1), (1, 0)])


def summands(value):
    axes = ("proto", "crop")
    count = lax.axis_size("proto") * lax.axis_size("crop")
    if count & (count - 1):
        return [lax.psum(value, axes)]
    parts = [value]
    stride = 1
    while stride < count:
        if stride > 1:
            parts = [functools.reduce(jnp.add, parts)]
        masks = [stride * k for k in (1, 2, 3) if stride * k < count]
        for mask in masks:
            pairs = [(place, place ^ mask) for place in range(count)]
            parts.append(lax.ppermute(parts[0], axes, pairs))
        stride *= 4
    return parts


def halving_masks(axis):
    count = lax.axis_size(axis)
    return [1 << bit for bit in range(count.bit_length() - 1)]


def is_power_of_two(count):
    return count & (count - 1) == 0


def flipped(value, axis, mask):
    return lax.ppermute(value, axis, [(p, p ^ mask) for p in range(lax.axis_size(axis))])


def bit_of(place, mask):
    return jnp.where((place & mask) != 0, 1, 0)


def scattered(value):
    count = lax.axis_size("proto")
    if not is_power_of_two(count):
        return lax.psum_scatter(value, ("crop", "proto"), scatter_dimension=0, tiled=True)
    width = value.shape[1]
    rows = value.shape[0] // 2 // count
    steps = [("crop", 1)] + [("proto", mask) for mask in halving_masks("proto")]
    for axis, mask in steps:
        bit = bit_of(lax.axis_index(axis), mask)
        low = value.shape[0] // 2 if axis == "crop" else rows
        halves = value.reshape(-1, 2, low, width)
        theirs = lax.dynamic_index_in_dim(halves, 1 - bit, 1, keepdims=False)
        mine = lax.dynamic_index_in_dim(halves, bit, 1, keepdims=False)
        got = flipped(theirs.reshape(-1, width), axis, mask)
        value = mine.reshape(-1, width) + got
    return value


def joined(mine, other, bit):
    return jnp.concatenate(
        [jnp.where(bit == 0, mine, other), jnp.where(bit == 0, other, mine)], axis=0
    )


def step(embeddings, weights):
    role_place = lax.axis_index("role")
    crop_place = lax.axis_index("crop")
    own_embed = embeddings[0]
    own_weight = weights[0]
    crops = 2 * own_embed.shape[0]
    depth = own_embed.shape[1]
    block_width = own_weight.shape[1]
    teaches = role_place == 0

    own_quarter = quarter_of(role_place, crop_place)
    partner_quarter = quarter_of(1 - role_place, crop_place)
    order = [own_quarter, own_quarter ^ 2, own_quarter ^ 1, own_quarter ^ 3]
    places = jnp.stack([role_place, own_quarter, partner_quarter, crop_place]).astype(jnp.int32)

    crop_embed = swapped(own_embed, "crop")
    arrived = []
    for chunk in range(SLICED):
        sent = columns_of(own_weight, chunk)
        arrived.append(swapped(sent, "role"))
    proto_place = lax.axis_index("proto")
    spread = is_power_of_two(lax.axis_size("proto"))
    masks = halving_masks("proto") if spread else []
    part_rows = own_embed.shape[0] // lax.axis_size("proto") if spread else own_embed.shape[0]
    part_start = part_rows * proto_place if spread else 0
    role_embed = swapped(lax.dynamic_slice_in_dim(own_embed, part_start, part_rows), "role")
    own_all = joined(own_embed, crop_embed, crop_place)

    scale = jnp.where(teaches, SHARPEN, SOFTEN).astype(jnp.float32).reshape(1)
    parts = []
    diagonal_embed = None
    for iteration in range(ITERS):
        if iteration == 0:
            row_sums, own_factor, partner_factor, powers, *columns = first_pass(
                places, scale, own_all, own_weight
            )
        else:
            row_sums, own_factor, partner_factor = later_pass(places, powers, parts)
        if iteration == 0:
            for chunk in range(SLICED, CHUNKS):
                arrived.append(swapped(columns[chunk - SLICED], "role"))
        parts = summands(row_sums)
        for place, mask in enumerate(masks):
            if min(max(place - 1, 0), ITERS - 1) != iteration:
                continue
            role_embed, _ = lax.optimization_barrier((role_embed, row_sums))
            got_embed = flipped(role_embed, "proto", mask)
            role_embed = joined(role_embed, got_embed, bit_of(proto_place, mask))

        if iteration == ITERS - 1:
            diagonal_embed = swapped(role_embed, "crop")
    role_embed, diagonal_embed, own_all, _ = lax.optimization_barrier(
        (role_embed, diagonal_embed, own_all, row_sums)
    )
    other_all = joined(role_embed, diagonal_embed, crop_place)
    blocks = jnp.where(teaches, other_all, own_all).T.reshape(4, depth // 4, crops)
    turned = jnp.concatenate(
        [lax.dynamic_index_in_dim(blocks, place, 0, keepdims=False) for place in order], axis=0
    )

    got_factor = swapped(partner_factor, "role")
    got_inverse = swapped(functools.reduce(jnp.add, parts), "role")
    row_scale, inverse_sum, columns = final_scales(
        places, parts, got_inverse, own_factor, got_factor, (turned, other_all)
    )

    embed_part = None
    result = None
    for chunk in GRAD_ORDER:
        kept_piece, crop_piece, role_piece, diagonal_piece, embed_part = gradients(
            places,
            chunk,
            other_all,
            turned,
            own_weight,
            arrived[chunk],
            powers,
            (row_scale, inverse_sum),
            columns,
            embed_part,
        )
        diagonal_piece = swapped(diagonal_piece, "role", "crop")
        role_piece = swapped(role_piece, "role")
        crop_piece = swapped(crop_piece, "crop")
        pieces = (kept_piece, crop_piece, role_piece, diagonal_piece)
        result = placed_pieces(chunk, pieces, result, block_width)
    weight_block = result.reshape(1, 1, depth // 4, block_width)

    summed = scattered(embed_part)
    sides = summed.reshape(summed.shape[0], 2, depth // 2)
    theirs = lax.dynamic_index_in_dim(sides, 1 - role_place, 1, keepdims=False)
    mine = lax.dynamic_index_in_dim(sides, role_place, 1, keepdims=False)
    got_side = swapped(theirs, "role")
    embed_block = (mine + got_side).astype(jnp.bfloat16)[None]
    return (weight_block, embed_block)


def solution(mesh):
    placed = (P("role", "crop", None), P("role", None, "proto"))
    return jax.shard_map(
        step,
        mesh=mesh,
        in_specs=placed,
        out_specs=(P("crop", "role", None, "proto"), P("crop", "proto", "role")),
        check_vma=False,
    )
```
